512 devices in a mesh: dp: 8 (over z), space: 64 (over y, x, core).
Axes of the slice: x: 4, y: 8, z: 8, core: 2. Of those that a mesh axis runs over, the one named last changes fastest.
Arguments:
- image: bfloat16 [8, 1024, 16, 512], P('dp', 'space'), may hold values from -6 to 6
- cotangent: bfloat16 [8, 1024, 4, 256], P('dp', 'space'), may hold values from -6 to 6
- live_count: int32 [8, 64], P('dp', 'space'), may hold values from 8 to 16, as said below
- neighbours: int32 [8, 1024, 8], P('dp', 'space'), may hold values from -1 to 1023, as said below
- weight_one: bfloat16 [3, 3, 32, 64], replicated, may hold values from -0.375 to 0.375
- weight_two: bfloat16 [3, 3, 64, 64], replicated, may hold values from -0.25 to 0.25
- gain_one: float32 [64], replicated, may hold values from 0.1 to 1.9
- gain_two: float32 [64], replicated, may hold values from 0.1 to 1.9
Outputs:
- grad_weight_one: float32 [3, 3, 32, 64], replicated
- grad_weight_two: float32 [3, 3, 64, 64], replicated
- grad_gain_one: float32 [64], replicated
- grad_gain_two: float32 [64], replicated
The draws below stay inside these ranges and needn't reach their ends.
Inputs may be any that keep to these rules, and one draw needn't show every extreme that they name: A device's tiles fill its first live_count slots; some device of each slide holds 16 tiles. Entry j of a slot lists the global slot (device index along space times 16 plus slot) of the tile in direction j of the order NW, N, NE, W, E, SW, S, SE, or -1 for background or the window's edge; rows of dead slots are all -1. Tiles are numbered in raster order within each device's band. A tile's neighbours above and below are on its own device; those to its left lie on its own device or the one before it along space, those to its right on its own device or the one after it.
All inputs are finite; a program needn't handle non-finite values.
Results may differ from the reference program's by a relative error of at most 0.0051.
Values may be sent and summed in bfloat16 or wider, within the bound.
A program may use at most 64 MiB of HBM per device.

```python
import math
import jax
import jax.numpy as jnp
from jax import lax

TILE = 16
TPD = 16
C0 = 32
C1 = 64
C2 = 64
GH = 20
BW = 2
SLIDES = 8
SLOTS = 1024
H1 = 8
H2 = 4


NEIGHBOUR_STEPS = ((-1, -1), (-1, 0), (-1, 1), (0, -1), (0, 1), (1, -1), (1, 0), (1, 1))


def slide_layout(slide_key):
    device_count = SLOTS // TPD
    cell_count = GH * BW
    key_count, key_full, key_cells = jax.random.split(slide_key, 3)
    counts = jax.random.randint(key_count, (device_count,), TPD // 2, TPD + 1)
    heaviest = jax.random.randint(key_full, (), 0, device_count)
    counts = jnp.where(jnp.arange(device_count) == heaviest, TPD, counts).astype(jnp.int32)
    randoms = jax.random.randint(key_cells, (device_count, cell_count), 0, 1 << 20)
    cell_index = jnp.arange(cell_count, dtype=jnp.int32)[None, :]
    scores = jnp.where(cell_index < BW, cell_index, randoms * cell_count + cell_index + cell_count)
    ordering = jnp.argsort(scores, axis=1, stable=True)
    cell_rank = jnp.argsort(ordering, axis=1, stable=True)
    tissue = cell_rank < counts[:, None]
    slot_index = jnp.cumsum(tissue.astype(jnp.int32), axis=1) - 1
    devices = jnp.arange(device_count, dtype=jnp.int32)[:, None]
    tile_ident = jnp.where(tissue, devices * TPD + slot_index, -1).astype(jnp.int32)
    width_all = device_count * BW
    tile_grid = tile_ident.reshape(device_count, GH, BW).transpose(1, 0, 2).reshape(GH, width_all)
    padded = jnp.pad(tile_grid, 1, constant_values=-1)
    nearby = jnp.stack([padded[1 + row_step:1 + row_step + GH, 1 + col_step:1 + col_step + width_all] for row_step, col_step in NEIGHBOUR_STEPS], axis=-1)
    nearby = jnp.where(tile_grid[:, :, None] >= 0, nearby, -1)
    target = jnp.where(tile_grid >= 0, tile_grid, SLOTS).reshape(-1)
    lookup = jnp.full((SLOTS, 8), -1, jnp.int32).at[target].set(nearby.reshape(-1, 8).astype(jnp.int32), mode='drop')
    return (counts, lookup)


def layout(key):
    slide_keys = jax.random.split(jax.random.fold_in(key, 11), SLIDES)
    return jax.vmap(slide_layout)(slide_keys)


def draw_live_count(key, part):
    return layout(key)[0]


def draw_neighbours(key, part):
    return layout(key)[1]


def shard_levels(rng, shape, shards, smallest, largest):
    level = 1.0
    for position, shards_of in shards:
        draws = jax.random.uniform(jax.random.fold_in(jax.random.fold_in(rng, 6), position), (shards_of,), jnp.float32, smallest / len(shards), largest / len(shards))
        level = level * jnp.repeat(jnp.exp(draws), shape[position] // shards_of).reshape((-1,) + (1,) * (len(shape) - 1 - position))
    return level


def bell_draw(stream_key, dims, width, most, cuts=(), kind=jnp.bfloat16):
    array = width * jax.random.normal(stream_key, dims, jnp.float32)
    if cuts:
        array = array * shard_levels(stream_key, dims, cuts, -0.22, 0.18)
    return jnp.clip(array, -most, most).astype(kind)


def setup_inputs(seed: int = 0) -> dict:
    arg_keys = jax.random.split(jax.random.key(seed), 9)
    return {
        "image": bell_draw(arg_keys[0], (SLIDES, SLOTS, TILE, TILE * C0), 1.0, 6.0, ((0, 8), (1, 64))),
        "cotangent": bell_draw(arg_keys[1], (SLIDES, SLOTS, H2, H2 * C2), 1.0, 6.0, ((0, 8), (1, 64))),
        "live_count": draw_live_count(jax.random.fold_in(arg_keys[8], 71), 0),
        "neighbours": draw_neighbours(jax.random.fold_in(arg_keys[8], 71), 0),
        "weight_one": bell_draw(arg_keys[4], (3, 3, C0, C1), (9 * C0) ** -0.5, 0.375),
        "weight_two": bell_draw(arg_keys[5], (3, 3, C1, C2), (9 * C1) ** -0.5, 0.25),
        "gain_one": jnp.clip(1.0 + 0.18 * jax.random.normal(arg_keys[6], (C1,), jnp.float32), 0.1, 1.9),
        "gain_two": jnp.clip(1.0 + 0.18 * jax.random.normal(arg_keys[7], (C2,), jnp.float32), 0.1, 1.9),
    }


EPS = 1e-05

def norm_forward(values):
    middle = lax.optimization_barrier(jnp.mean(values, axis=-1, keepdims=True))
    centred = values - middle
    inverse = lax.rsqrt(lax.optimization_barrier(jnp.mean(centred * centred, axis=-1, keepdims=True)) + EPS)
    return (centred * inverse, inverse)

def norm_backward(grad_act, hidden, normed, inverse, gain):
    sig = jax.nn.sigmoid(hidden)
    grad_hidden = grad_act * sig * (1.0 + hidden * (1.0 - sig))
    grad_gain = lax.optimization_barrier(jnp.sum(grad_hidden * normed, axis=(0, 1, 2)))
    scaled = grad_hidden * gain
    centre = lax.optimization_barrier(jnp.mean(scaled, axis=-1, keepdims=True))
    along = lax.optimization_barrier(jnp.mean(scaled * normed, axis=-1, keepdims=True))
    return (inverse * (scaled - centre - normed * along), grad_gain)

def pick_rows(source, idents):
    safe = jnp.maximum(idents, 0).astype(jnp.int32)
    picked = source[safe]
    shape_mask = (idents >= 0).reshape((-1,) + (1,) * (picked.ndim - 1))
    return jnp.where(shape_mask, picked, jnp.zeros_like(picked))

def pad_field(field, nearby):
    south_rows = pick_rows(field[:, 0], nearby[:, 6])
    east_cols = pick_rows(field[:, :, 0], nearby[:, 4])
    corners = pick_rows(field[:, 0, 0], nearby[:, 7])
    lower = jnp.concatenate([field, south_rows[:, None]], axis=1)
    right = jnp.concatenate([east_cols, corners[:, None]], axis=1)
    return jnp.concatenate([lower, right[:, :, None]], axis=2)

def conv_forward(padded, weight):
    return lax.conv_general_dilated(padded.astype(jnp.float32), weight.astype(jnp.float32), (2, 2), 'VALID', dimension_numbers=('NHWC', 'HWIO', 'NHWC'), precision=lax.Precision.HIGHEST)

def weight_grad(padded, grad_z):
    size = grad_z.shape[1]
    wide = padded.astype(jnp.float32)
    grads = grad_z.astype(jnp.float32)
    blocks = []
    for row_off in range(3):
        line = []
        for col_off in range(3):
            window = wide[:, row_off:row_off + 2 * size:2, col_off:col_off + 2 * size:2, :]
            line.append(jnp.einsum('nijc,nijo->co', window, grads, precision=lax.Precision.HIGHEST))
        blocks.append(jnp.stack(line))
    return jnp.stack(blocks)

def input_grad(grad_z, weight):
    size = grad_z.shape[1]
    grads = grad_z.astype(jnp.float32)
    wide = weight.astype(jnp.float32)
    total = jnp.zeros((grad_z.shape[0], 2 * size + 1, 2 * size + 1, weight.shape[2]), jnp.float32)
    for row_off in range(3):
        for col_off in range(3):
            term = jnp.einsum('nijo,co->nijc', grads, wide[row_off, col_off], precision=lax.Precision.HIGHEST)
            total = total.at[:, row_off:row_off + 2 * size:2, col_off:col_off + 2 * size:2, :].add(term)
    return total

def slide_grads(image, cotangent, counts, nearby, weight_one, weight_two, gain_one, gain_two):
    slot_ids = jnp.arange(SLOTS, dtype=jnp.int32)
    live = slot_ids % TPD < counts[slot_ids // TPD]
    field = image.reshape(SLOTS, TILE, TILE, C0)
    field = jnp.where(live[:, None, None, None], field, jnp.zeros_like(field))
    padded_one = pad_field(field, nearby)
    normed_one, inverse_one = norm_forward(conv_forward(padded_one, weight_one))
    hidden_one = normed_one * gain_one
    act_one = jax.nn.silu(hidden_one).astype(jnp.bfloat16)
    padded_two = pad_field(act_one, nearby)
    normed_two, inverse_two = norm_forward(conv_forward(padded_two, weight_two))
    hidden_two = normed_two * gain_two
    factor = 1.0 / math.sqrt(SLIDES * SLOTS * H2 * H2)
    grad_out = cotangent.reshape(SLOTS, H2, H2, C2).astype(jnp.float32)
    grad_out = jnp.where(live[:, None, None, None], grad_out * factor, jnp.zeros_like(grad_out))
    grad_z_two, grad_gain_two = norm_backward(grad_out, hidden_two, normed_two, inverse_two, gain_two)
    grad_z_two = grad_z_two.astype(jnp.bfloat16)
    grad_weight_two = weight_grad(padded_two, grad_z_two)
    grad_padded = input_grad(grad_z_two, weight_two)
    bottom = grad_padded[:, H1, :H1, :].astype(jnp.bfloat16)
    right = grad_padded[:, :, H1, :].astype(jnp.bfloat16)
    grad_act = grad_padded[:, :H1, :H1, :]
    grad_act = grad_act.at[:, 0].add(pick_rows(bottom, nearby[:, 1]).astype(jnp.float32))
    grad_act = grad_act.at[:, :, 0].add(pick_rows(right[:, :H1], nearby[:, 3]).astype(jnp.float32))
    grad_act = grad_act.at[:, 0, 0].add(pick_rows(right[:, H1], nearby[:, 0]).astype(jnp.float32))
    grad_z_one, grad_gain_one = norm_backward(grad_act, hidden_one, normed_one, inverse_one, gain_one)
    grad_weight_one = weight_grad(padded_one, grad_z_one.astype(jnp.bfloat16))
    return (grad_weight_one, grad_weight_two, grad_gain_one, grad_gain_two)

def reference(image, cotangent, live_count, neighbours, weight_one, weight_two, gain_one, gain_two):

    def per_slide(inputs):
        return slide_grads(inputs[0], inputs[1], inputs[2], inputs[3], weight_one, weight_two, gain_one, gain_two)
    results = lax.map(per_slide, (image, cotangent, live_count, neighbours))
    return (lax.optimization_barrier(jnp.sum(results[0], axis=0)), lax.optimization_barrier(jnp.sum(results[1], axis=0)), lax.optimization_barrier(jnp.sum(results[2], axis=0)), lax.optimization_barrier(jnp.sum(results[3], axis=0)))
```

```python
import math

import jax
import jax.numpy as jnp
from jax import lax
from jax.sharding import Mesh
from jax.sharding import PartitionSpec as P

SPACE = ("space_0", "space_1", "space_2")


EPS = 1e-05


def from_behind(value, axis, steps):
    count = lax.axis_size(axis)
    first, last = (max(0, -steps), min(count, count - steps))
    return lax.ppermute(value, axis, [(source, source + steps) for source in range(first, last)])


def cut_along(value, dim, peers):
    before, after = (value.shape[:dim], value.shape[dim + 1 :])
    return jnp.moveaxis(value.reshape(*before, peers, -1, *after), dim, 0)


def sent_and_summed(value, axis, dim):
    peers = lax.axis_size(axis)
    pieces = lax.all_to_all(cut_along(value, dim, peers), axis, 0, 0, tiled=True)
    return jnp.sum(pieces, axis=0)


def summed_rows(value, axes, dim):
    far, near = axes
    pieces = cut_along(value, dim, lax.axis_size(far))
    nearer = sent_and_summed(pieces, near, dim + 1)
    arrived = lax.all_to_all(nearer, far, split_axis=0, concat_axis=0, tiled=True)
    return arrived.sum(axis=0)


def rows_for(lines, peers):
    spare = -lines.shape[0] % peers
    if not spare:
        return lines
    return jnp.concatenate([lines, jnp.zeros((spare, *lines.shape[1:]), lines.dtype)])


def from_everyone(value, axis):
    peers = lax.axis_size(axis)
    return lax.all_to_all(
        jnp.broadcast_to(value[None], (peers, *value.shape)), axis, 0, 0, tiled=True
    )


def in_order(pieces, dim):
    pieces = jnp.moveaxis(pieces, 0, dim)
    dims = pieces.shape
    return pieces.reshape(*dims[:dim], dims[dim] * dims[dim + 1], *dims[dim + 2 :])


def gathered_by_axis(value, axes, dim):
    far, near = axes
    first = from_everyone(value, far)
    pieces = jnp.swapaxes(from_everyone(first, near), 0, 1)
    return in_order(pieces.reshape(-1, *value.shape), dim)


def total_of(value, axes):
    lines = value.reshape(-1)
    own = summed_rows(rows_for(lines, lax.axis_size(axes[0]) * lax.axis_size(axes[1])), axes, 0)
    whole = gathered_by_axis(own, axes, 0)
    return whole[: len(lines)].reshape(value.shape)


def norm_forward(values):
    middle = jnp.mean(values, axis=-1, keepdims=True)
    centred = values - middle
    inverse = lax.rsqrt(jnp.mean(centred * centred, axis=-1, keepdims=True) + EPS)
    return (centred * inverse, inverse)


def norm_backward(grad_act, hidden, normed, inverse, gain):
    sig = jax.nn.sigmoid(hidden)
    grad_hidden = grad_act * sig * (1.0 + hidden * (1.0 - sig))
    grad_gain = jnp.sum(grad_hidden * normed, axis=(0, 1, 2))
    scaled = grad_hidden * gain
    centre = jnp.mean(scaled, axis=-1, keepdims=True)
    along = jnp.mean(scaled * normed, axis=-1, keepdims=True)
    return (inverse * (scaled - centre - normed * along), grad_gain)


def select_rows(source, idents, offset):
    positions = jnp.clip(idents - offset, 0, source.shape[0] - 1)
    picked = jnp.take(source, positions, axis=0)
    return jnp.where((idents >= 0)[:, None], picked, jnp.zeros_like(picked))


def assemble(field, south_rows, east_cols, corners):
    lower = jnp.concatenate([field, south_rows[:, None]], axis=1)
    right = jnp.concatenate([east_cols, corners[:, None]], axis=1)
    return jnp.concatenate([lower, right[:, :, None]], axis=2)


def conv_forward(padded, weight):
    return lax.conv_general_dilated(
        padded,
        weight,
        (2, 2),
        "VALID",
        dimension_numbers=("NHWC", "HWIO", "NHWC"),
        preferred_element_type=jnp.float32,
    )


def weight_grad(padded, grad_z):
    size = grad_z.shape[1]
    blocks = []
    for row_off in range(3):
        line = []
        for col_off in range(3):
            window = padded[
                :, row_off : row_off + 2 * size : 2, col_off : col_off + 2 * size : 2, :
            ]
            line.append(
                jnp.einsum("nijc,nijo->co", window, grad_z, preferred_element_type=jnp.float32)
            )
        blocks.append(jnp.stack(line))
    return jnp.stack(blocks)


def input_grad(grad_z, weight):
    size = grad_z.shape[1]
    total = jnp.zeros((grad_z.shape[0], 2 * size + 1, 2 * size + 1, weight.shape[2]), jnp.float32)
    for row_off in range(3):
        for col_off in range(3):
            term = jnp.einsum(
                "nijo,co->nijc",
                grad_z,
                weight[row_off, col_off],
                preferred_element_type=jnp.float32,
            )
            total = total.at[
                :, row_off : row_off + 2 * size : 2, col_off : col_off + 2 * size : 2, :
            ].add(term)
    return total


def on_device(image, cotangent, live_count, neighbours, weight_one, weight_two, gain_one, gain_two):
    slots = image.shape[1]
    tile = image.shape[2]
    chan_in = weight_one.shape[2]
    chan_mid = weight_one.shape[3]
    chan_out = weight_two.shape[3]
    half = tile // 2
    quarter = tile // 4
    offset = lax.axis_index(SPACE) * slots
    nearby = neighbours[0]
    live = jnp.arange(slots) < live_count[0, 0]
    field = image[0].reshape(slots, tile, tile, chan_in)
    field = jnp.where(live[:, None, None, None], field, jnp.zeros_like(field))
    south_image = select_rows(field[:, 0].reshape(slots, tile * chan_in), nearby[:, 6], offset)
    image_cols = field[:, :, 0, :].reshape(slots, tile * chan_in)
    following = from_behind(image_cols, SPACE, -1)
    source = jnp.concatenate([image_cols, following], axis=0)
    east_image = select_rows(source, nearby[:, 4], offset)
    diag_image = select_rows(source, nearby[:, 7], offset)
    padded_one = assemble(
        field,
        south_image.reshape(slots, tile, chan_in),
        east_image.reshape(slots, tile, chan_in),
        diag_image[:, :chan_in],
    )
    normed_one, inverse_one = norm_forward(conv_forward(padded_one, weight_one))
    hidden_one = normed_one * gain_one
    act_one = jax.nn.silu(hidden_one).astype(jnp.bfloat16)
    south_act = select_rows(act_one[:, 0].reshape(slots, half * chan_mid), nearby[:, 6], offset)
    act_cols = act_one[:, :, 0, :].reshape(slots, half * chan_mid)
    act_following = from_behind(act_cols, SPACE, -1)
    act_source = jnp.concatenate([act_cols, act_following], axis=0)
    east_act = select_rows(act_source, nearby[:, 4], offset)
    diag_act = select_rows(act_source, nearby[:, 7], offset)
    padded_two = assemble(
        act_one,
        south_act.reshape(slots, half, chan_mid),
        east_act.reshape(slots, half, chan_mid),
        diag_act[:, :chan_mid],
    )
    normed_two, inverse_two = norm_forward(conv_forward(padded_two, weight_two))
    hidden_two = normed_two * gain_two
    factor = 1.0 / math.sqrt(lax.axis_size("dp") * lax.axis_size(SPACE) * slots * quarter * quarter)
    grad_out = cotangent[0].reshape(slots, quarter, quarter, chan_out).astype(jnp.float32)
    grad_out = jnp.where(live[:, None, None, None], grad_out * factor, jnp.zeros_like(grad_out))
    grad_z_two, grad_gain_two = norm_backward(
        grad_out, hidden_two, normed_two, inverse_two, gain_two
    )
    grad_z_two = grad_z_two.astype(jnp.bfloat16)
    grad_weight_two = weight_grad(padded_two, grad_z_two)
    grad_padded = input_grad(grad_z_two, weight_two)
    bottom = grad_padded[:, half, :half, :].astype(jnp.bfloat16).reshape(slots, half * chan_mid)
    right = grad_padded[:, :, half, :].astype(jnp.bfloat16).reshape(slots, (half + 1) * chan_mid)
    from_north = select_rows(bottom, nearby[:, 1], offset).reshape(slots, half, chan_mid)
    previous = from_behind(right, SPACE, 1)
    rim_source = jnp.concatenate([previous, right], axis=0)
    from_west = select_rows(rim_source, nearby[:, 3], offset - slots).reshape(
        slots, half + 1, chan_mid
    )
    from_diag = select_rows(rim_source, nearby[:, 0], offset - slots).reshape(
        slots, half + 1, chan_mid
    )
    grad_act = grad_padded[:, :half, :half, :]
    grad_act = grad_act.at[:, 0].add(from_north.astype(jnp.float32))
    grad_act = grad_act.at[:, :, 0].add(from_west[:, :half].astype(jnp.float32))
    grad_act = grad_act.at[:, 0, 0].add(from_diag[:, half].astype(jnp.float32))
    grad_z_one, grad_gain_one = norm_backward(
        grad_act, hidden_one, normed_one, inverse_one, gain_one
    )
    grad_weight_one = weight_grad(padded_one, grad_z_one.astype(jnp.bfloat16))
    parts = (grad_weight_one, grad_weight_two, grad_gain_one, grad_gain_two)
    flat = jnp.concatenate([part.reshape(-1) for part in parts])
    flat = lax.psum(flat, ("dp", "space_0", "space_1", "space_2"))
    sizes = [part.size for part in parts]
    bounds = [sum(sizes[:index]) for index in range(len(sizes) + 1)]
    grad_weight_one, grad_weight_two, grad_gain_one, grad_gain_two = (
        flat[start:end].reshape(part.shape)
        for start, end, part in zip(bounds[:-1], bounds[1:], parts)
    )
    return (grad_weight_one, grad_weight_two, grad_gain_one, grad_gain_two)


def solution(mesh):
    torus = Mesh(
        mesh.devices.reshape(mesh.shape["dp"], 8, 4, 2), ("dp", "space_0", "space_1", "space_2")
    )
    return jax.shard_map(
        on_device,
        mesh=torus,
        in_specs=(
            P("dp", SPACE, None, None),
            P("dp", SPACE, None, None),
            P("dp", SPACE),
            P("dp", SPACE, None),
            P(),
            P(),
            P(),
            P(),
        ),
        out_specs=(P(), P(), P(), P()),
        check_vma=False,
    )
```

```python
import math

import jax
import jax.numpy as jnp
from jax import lax
from jax.sharding import Mesh
from jax.sharding import PartitionSpec as P

SPACE = ("space_0", "space_1", "space_2")


EPS = 1e-05


def from_behind(value, axis, steps):
    count = lax.axis_size(axis)
    first, last = (max(0, -steps), min(count, count - steps))
    return lax.ppermute(value, axis, [(source, source + steps) for source in range(first, last)])


def cut_along(value, dim, peers):
    before, after = (value.shape[:dim], value.shape[dim + 1 :])
    return jnp.moveaxis(value.reshape(*before, peers, -1, *after), dim, 0)


def sent_and_summed(value, axis, dim):
    peers = lax.axis_size(axis)
    pieces = lax.all_to_all(cut_along(value, dim, peers), axis, 0, 0, tiled=True)
    return jnp.sum(pieces, axis=0)


def summed_rows(value, axes, dim):
    far, near = axes
    pieces = cut_along(value, dim, lax.axis_size(far))
    nearer = sent_and_summed(pieces, near, dim + 1)
    arrived = lax.all_to_all(nearer, far, split_axis=0, concat_axis=0, tiled=True)
    return arrived.sum(axis=0)


def rows_for(lines, peers):
    spare = -lines.shape[0] % peers
    if not spare:
        return lines
    return jnp.concatenate([lines, jnp.zeros((spare, *lines.shape[1:]), lines.dtype)])


def from_everyone(value, axis):
    peers = lax.axis_size(axis)
    return lax.all_to_all(
        jnp.broadcast_to(value[None], (peers, *value.shape)), axis, 0, 0, tiled=True
    )


def in_order(pieces, dim):
    pieces = jnp.moveaxis(pieces, 0, dim)
    dims = pieces.shape
    return pieces.reshape(*dims[:dim], dims[dim] * dims[dim + 1], *dims[dim + 2 :])


def gathered_by_axis(value, axes, dim):
    far, near = axes
    first = from_everyone(value, far)
    pieces = jnp.swapaxes(from_everyone(first, near), 0, 1)
    return in_order(pieces.reshape(-1, *value.shape), dim)


def total_of(value, axes):
    lines = value.reshape(-1)
    own = summed_rows(rows_for(lines, lax.axis_size(axes[0]) * lax.axis_size(axes[1])), axes, 0)
    whole = gathered_by_axis(own, axes, 0)
    return whole[: len(lines)].reshape(value.shape)


def norm_forward(values):
    middle = jnp.mean(values, axis=-1, keepdims=True)
    centred = values - middle
    inverse = lax.rsqrt(jnp.mean(centred * centred, axis=-1, keepdims=True) + EPS)
    return (centred * inverse, inverse)


def norm_backward(grad_act, hidden, normed, inverse, gain):
    sig = jax.nn.sigmoid(hidden)
    grad_hidden = grad_act * sig * (1.0 + hidden * (1.0 - sig))
    grad_gain = jnp.sum(grad_hidden * normed, axis=(0, 1, 2))
    scaled = grad_hidden * gain
    centre = jnp.mean(scaled, axis=-1, keepdims=True)
    along = jnp.mean(scaled * normed, axis=-1, keepdims=True)
    return (inverse * (scaled - centre - normed * along), grad_gain)


def select_rows(source, idents, offset):
    positions = jnp.clip(idents - offset, 0, source.shape[0] - 1)
    picked = jnp.take(source, positions, axis=0)
    return jnp.where((idents >= 0)[:, None], picked, jnp.zeros_like(picked))


def assemble(field, south_rows, east_cols, corners):
    lower = jnp.concatenate([field, south_rows[:, None]], axis=1)
    right = jnp.concatenate([east_cols, corners[:, None]], axis=1)
    return jnp.concatenate([lower, right[:, :, None]], axis=2)


def conv_forward(padded, weight):
    return lax.conv_general_dilated(
        padded,
        weight,
        (2, 2),
        "VALID",
        dimension_numbers=("NHWC", "HWIO", "NHWC"),
        preferred_element_type=jnp.float32,
    )


def weight_grad(padded, grad_z):
    size = grad_z.shape[1]
    blocks = []
    for row_off in range(3):
        line = []
        for col_off in range(3):
            window = padded[
                :, row_off : row_off + 2 * size : 2, col_off : col_off + 2 * size : 2, :
            ]
            line.append(
                jnp.einsum("nijc,nijo->co", window, grad_z, preferred_element_type=jnp.float32)
            )
        blocks.append(jnp.stack(line))
    return jnp.stack(blocks)


def input_grad(grad_z, weight):
    size = grad_z.shape[1]
    total = jnp.zeros((grad_z.shape[0], 2 * size + 1, 2 * size + 1, weight.shape[2]), jnp.float32)
    for row_off in range(3):
        for col_off in range(3):
            term = jnp.einsum(
                "nijo,co->nijc",
                grad_z,
                weight[row_off, col_off],
                preferred_element_type=jnp.float32,
            )
            total = total.at[
                :, row_off : row_off + 2 * size : 2, col_off : col_off + 2 * size : 2, :
            ].add(term)
    return total


def on_device(image, cotangent, live_count, neighbours, weight_one, weight_two, gain_one, gain_two):
    slots = image.shape[1]
    tile = image.shape[2]
    chan_in = weight_one.shape[2]
    chan_mid = weight_one.shape[3]
    chan_out = weight_two.shape[3]
    half = tile // 2
    quarter = tile // 4
    offset = lax.axis_index(SPACE) * slots
    nearby = neighbours[0]
    live = jnp.arange(slots) < live_count[0, 0]
    field = image[0].reshape(slots, tile, tile, chan_in)
    field = jnp.where(live[:, None, None, None], field, jnp.zeros_like(field))
    south_image = select_rows(field[:, 0].reshape(slots, tile * chan_in), nearby[:, 6], offset)
    image_cols = field[:, :, 0, :].reshape(slots, tile * chan_in)
    following = from_behind(image_cols, SPACE, -1)
    source = jnp.concatenate([image_cols, following], axis=0)
    east_image = select_rows(source, nearby[:, 4], offset)
    diag_image = select_rows(source, nearby[:, 7], offset)
    padded_one = assemble(
        field,
        south_image.reshape(slots, tile, chan_in),
        east_image.reshape(slots, tile, chan_in),
        diag_image[:, :chan_in],
    )
    normed_one, inverse_one = norm_forward(conv_forward(padded_one, weight_one))
    hidden_one = normed_one * gain_one
    act_one = jax.nn.silu(hidden_one).astype(jnp.bfloat16)
    south_act = select_rows(act_one[:, 0].reshape(slots, half * chan_mid), nearby[:, 6], offset)
    act_cols = act_one[:, :, 0, :].reshape(slots, half * chan_mid)
    act_following = from_behind(act_cols, SPACE, -1)
    act_source = jnp.concatenate([act_cols, act_following], axis=0)
    east_act = select_rows(act_source, nearby[:, 4], offset)
    diag_act = select_rows(act_source, nearby[:, 7], offset)
    padded_two = assemble(
        act_one,
        south_act.reshape(slots, half, chan_mid),
        east_act.reshape(slots, half, chan_mid),
        diag_act[:, :chan_mid],
    )
    normed_two, inverse_two = norm_forward(conv_forward(padded_two, weight_two))
    hidden_two = normed_two * gain_two
    factor = 1.0 / math.sqrt(lax.axis_size("dp") * lax.axis_size(SPACE) * slots * quarter * quarter)
    grad_out = cotangent[0].reshape(slots, quarter, quarter, chan_out).astype(jnp.float32)
    grad_out = jnp.where(live[:, None, None, None], grad_out * factor, jnp.zeros_like(grad_out))
    grad_z_two, grad_gain_two = norm_backward(
        grad_out, hidden_two, normed_two, inverse_two, gain_two
    )
    grad_z_two = grad_z_two.astype(jnp.bfloat16)
    grad_weight_two = weight_grad(padded_two, grad_z_two)
    grad_padded = input_grad(grad_z_two, weight_two)
    bottom = grad_padded[:, half, :half, :].astype(jnp.bfloat16).reshape(slots, half * chan_mid)
    right = grad_padded[:, :, half, :].astype(jnp.bfloat16).reshape(slots, (half + 1) * chan_mid)
    from_north = select_rows(bottom, nearby[:, 1], offset).reshape(slots, half, chan_mid)
    previous = from_behind(right, SPACE, 1)
    rim_source = jnp.concatenate([previous, right], axis=0)
    from_west = select_rows(rim_source, nearby[:, 3], offset - slots).reshape(
        slots, half + 1, chan_mid
    )
    from_diag = select_rows(rim_source, nearby[:, 0], offset - slots).reshape(
        slots, half + 1, chan_mid
    )
    grad_act = grad_padded[:, :half, :half, :]
    grad_act = grad_act.at[:, 0].add(from_north.astype(jnp.float32))
    grad_act = grad_act.at[:, :, 0].add(from_west[:, :half].astype(jnp.float32))
    grad_act = grad_act.at[:, 0, 0].add(from_diag[:, half].astype(jnp.float32))
    grad_z_one, grad_gain_one = norm_backward(
        grad_act, hidden_one, normed_one, inverse_one, gain_one
    )
    grad_weight_one = weight_grad(padded_one, grad_z_one.astype(jnp.bfloat16))
    parts = (grad_weight_one, grad_weight_two, grad_gain_one, grad_gain_two)
    flat = jnp.concatenate([part.reshape(-1) for part in parts])
    flat = total_of(flat, (("dp", "space_0"), ("space_1", "space_2")))
    sizes = [part.size for part in parts]
    bounds = [sum(sizes[:index]) for index in range(len(sizes) + 1)]
    grad_weight_one, grad_weight_two, grad_gain_one, grad_gain_two = (
        flat[start:end].reshape(part.shape)
        for start, end, part in zip(bounds[:-1], bounds[1:], parts)
    )
    return (grad_weight_one, grad_weight_two, grad_gain_one, grad_gain_two)


def solution(mesh):
    torus = Mesh(
        mesh.devices.reshape(mesh.shape["dp"], 8, 4, 2), ("dp", "space_0", "space_1", "space_2")
    )
    return jax.shard_map(
        on_device,
        mesh=torus,
        in_specs=(
            P("dp", SPACE, None, None),
            P("dp", SPACE, None, None),
            P("dp", SPACE),
            P("dp", SPACE, None),
            P(),
            P(),
            P(),
            P(),
        ),
        out_specs=(P(), P(), P(), P()),
        check_vma=False,
    )
```

```python
import math

import jax
import jax.numpy as jnp
from jax import lax
from jax.sharding import Mesh
from jax.sharding import PartitionSpec as P

SPACE = ("space_0", "space_1", "space_2")


EPS = 1e-05


def from_behind(value, axis, steps):
    count = lax.axis_size(axis)
    first, last = (max(0, -steps), min(count, count - steps))
    return lax.ppermute(value, axis, [(source, source + steps) for source in range(first, last)])


def cut_along(value, dim, peers):
    before, after = (value.shape[:dim], value.shape[dim + 1 :])
    return jnp.moveaxis(value.reshape(*before, peers, -1, *after), dim, 0)


def sent_and_summed(value, axis, dim):
    peers = lax.axis_size(axis)
    pieces = lax.all_to_all(cut_along(value, dim, peers), axis, 0, 0, tiled=True)
    return jnp.sum(pieces, axis=0)


def summed_rows(value, axes, dim):
    far, near = axes
    pieces = cut_along(value, dim, lax.axis_size(far))
    nearer = sent_and_summed(pieces, near, dim + 1)
    arrived = lax.all_to_all(nearer, far, split_axis=0, concat_axis=0, tiled=True)
    return arrived.sum(axis=0)


def rows_for(lines, peers):
    spare = -lines.shape[0] % peers
    if not spare:
        return lines
    return jnp.concatenate([lines, jnp.zeros((spare, *lines.shape[1:]), lines.dtype)])


def from_everyone(value, axis):
    peers = lax.axis_size(axis)
    return lax.all_to_all(
        jnp.broadcast_to(value[None], (peers, *value.shape)), axis, 0, 0, tiled=True
    )


def in_order(pieces, dim):
    pieces = jnp.moveaxis(pieces, 0, dim)
    dims = pieces.shape
    return pieces.reshape(*dims[:dim], dims[dim] * dims[dim + 1], *dims[dim + 2 :])


def gathered_by_axis(value, axes, dim):
    far, near = axes
    first = from_everyone(value, far)
    pieces = jnp.swapaxes(from_everyone(first, near), 0, 1)
    return in_order(pieces.reshape(-1, *value.shape), dim)


def total_of(value, axes):
    lines = value.reshape(-1)
    own = summed_rows(rows_for(lines, lax.axis_size(axes[0]) * lax.axis_size(axes[1])), axes, 0)
    whole = gathered_by_axis(own, axes, 0)
    return whole[: len(lines)].reshape(value.shape)


def norm_forward(values):
    middle = jnp.mean(values, axis=-1, keepdims=True)
    centred = values - middle
    inverse = lax.rsqrt(jnp.mean(centred * centred, axis=-1, keepdims=True) + EPS)
    return (centred * inverse, inverse)


def norm_backward(grad_act, hidden, normed, inverse, gain):
    sig = jax.nn.sigmoid(hidden)
    grad_hidden = grad_act * sig * (1.0 + hidden * (1.0 - sig))
    grad_gain = jnp.sum(grad_hidden * normed, axis=(0, 1, 2))
    scaled = grad_hidden * gain
    centre = jnp.mean(scaled, axis=-1, keepdims=True)
    along = jnp.mean(scaled * normed, axis=-1, keepdims=True)
    return (inverse * (scaled - centre - normed * along), grad_gain)


def select_rows(source, idents, offset):
    positions = jnp.clip(idents - offset, 0, source.shape[0] - 1)
    picked = jnp.take(source, positions, axis=0)
    return jnp.where((idents >= 0)[:, None], picked, jnp.zeros_like(picked))


def assemble(field, south_rows, east_cols, corners):
    lower = jnp.concatenate([field, south_rows[:, None]], axis=1)
    right = jnp.concatenate([east_cols, corners[:, None]], axis=1)
    return jnp.concatenate([lower, right[:, :, None]], axis=2)


def conv_forward(padded, weight):
    return lax.conv_general_dilated(
        padded,
        weight,
        (2, 2),
        "VALID",
        dimension_numbers=("NHWC", "HWIO", "NHWC"),
        preferred_element_type=jnp.float32,
    )


def weight_grad(padded, grad_z):
    return lax.conv_general_dilated(
        padded,
        grad_z,
        (1, 1),
        "VALID",
        rhs_dilation=(2, 2),
        dimension_numbers=("CHWN", "IHWO", "HWNC"),
        preferred_element_type=jnp.float32,
    )


def input_grad(grad_z, weight):
    return lax.conv_general_dilated(
        grad_z,
        weight[::-1, ::-1],
        (1, 1),
        ((2, 2), (2, 2)),
        lhs_dilation=(2, 2),
        dimension_numbers=("NHWC", "HWOI", "NHWC"),
        preferred_element_type=jnp.float32,
    )


def on_device(image, cotangent, live_count, neighbours, weight_one, weight_two, gain_one, gain_two):
    slots = image.shape[1]
    tile = image.shape[2]
    chan_in = weight_one.shape[2]
    chan_mid = weight_one.shape[3]
    chan_out = weight_two.shape[3]
    half = tile // 2
    quarter = tile // 4
    offset = lax.axis_index(SPACE) * slots
    nearby = neighbours[0]
    live = jnp.arange(slots) < live_count[0, 0]
    field = image[0].reshape(slots, tile, tile, chan_in)
    field = jnp.where(live[:, None, None, None], field, jnp.zeros_like(field))
    south_image = select_rows(field[:, 0].reshape(slots, tile * chan_in), nearby[:, 6], offset)
    image_cols = field[:, :, 0, :].reshape(slots, tile * chan_in)
    following = from_behind(image_cols, SPACE, -1)
    source = jnp.concatenate([image_cols, following], axis=0)
    east_image = select_rows(source, nearby[:, 4], offset)
    diag_image = select_rows(source, nearby[:, 7], offset)
    padded_one = assemble(
        field,
        south_image.reshape(slots, tile, chan_in),
        east_image.reshape(slots, tile, chan_in),
        diag_image[:, :chan_in],
    )
    normed_one, inverse_one = norm_forward(conv_forward(padded_one, weight_one))
    hidden_one = normed_one * gain_one
    act_one = jax.nn.silu(hidden_one).astype(jnp.bfloat16)
    south_act = select_rows(act_one[:, 0].reshape(slots, half * chan_mid), nearby[:, 6], offset)
    act_cols = act_one[:, :, 0, :].reshape(slots, half * chan_mid)
    act_following = from_behind(act_cols, SPACE, -1)
    act_source = jnp.concatenate([act_cols, act_following], axis=0)
    east_act = select_rows(act_source, nearby[:, 4], offset)
    diag_act = select_rows(act_source, nearby[:, 7], offset)
    padded_two = assemble(
        act_one,
        south_act.reshape(slots, half, chan_mid),
        east_act.reshape(slots, half, chan_mid),
        diag_act[:, :chan_mid],
    )
    normed_two, inverse_two = norm_forward(conv_forward(padded_two, weight_two))
    hidden_two = normed_two * gain_two
    factor = 1.0 / math.sqrt(lax.axis_size("dp") * lax.axis_size(SPACE) * slots * quarter * quarter)
    grad_out = cotangent[0].reshape(slots, quarter, quarter, chan_out).astype(jnp.float32)
    grad_out = jnp.where(live[:, None, None, None], grad_out * factor, jnp.zeros_like(grad_out))
    grad_z_two, grad_gain_two = norm_backward(
        grad_out, hidden_two, normed_two, inverse_two, gain_two
    )
    grad_z_two = grad_z_two.astype(jnp.bfloat16)
    grad_weight_two = weight_grad(padded_two, grad_z_two)
    grad_padded = input_grad(grad_z_two, weight_two)
    bottom = grad_padded[:, half, :half, :].astype(jnp.bfloat16).reshape(slots, half * chan_mid)
    right = grad_padded[:, :, half, :].astype(jnp.bfloat16).reshape(slots, (half + 1) * chan_mid)
    from_north = select_rows(bottom, nearby[:, 1], offset).reshape(slots, half, chan_mid)
    previous = from_behind(right, SPACE, 1)
    rim_source = jnp.concatenate([previous, right], axis=0)
    from_west = select_rows(rim_source, nearby[:, 3], offset - slots).reshape(
        slots, half + 1, chan_mid
    )
    from_diag = select_rows(rim_source, nearby[:, 0], offset - slots).reshape(
        slots, half + 1, chan_mid
    )
    grad_act = grad_padded[:, :half, :half, :]
    grad_act = grad_act.at[:, 0].add(from_north.astype(jnp.float32))
    grad_act = grad_act.at[:, :, 0].add(from_west[:, :half].astype(jnp.float32))
    grad_act = grad_act.at[:, 0, 0].add(from_diag[:, half].astype(jnp.float32))
    grad_z_one, grad_gain_one = norm_backward(
        grad_act, hidden_one, normed_one, inverse_one, gain_one
    )
    grad_weight_one = weight_grad(padded_one, grad_z_one.astype(jnp.bfloat16))
    parts = (grad_weight_one, grad_weight_two, grad_gain_one, grad_gain_two)
    flat = jnp.concatenate([part.reshape(-1) for part in parts])
    flat = total_of(flat, (("dp", "space_0"), ("space_1", "space_2")))
    sizes = [part.size for part in parts]
    bounds = [sum(sizes[:index]) for index in range(len(sizes) + 1)]
    grad_weight_one, grad_weight_two, grad_gain_one, grad_gain_two = (
        flat[start:end].reshape(part.shape)
        for start, end, part in zip(bounds[:-1], bounds[1:], parts)
    )
    return (grad_weight_one, grad_weight_two, grad_gain_one, grad_gain_two)


def solution(mesh):
    torus = Mesh(
        mesh.devices.reshape(mesh.shape["dp"], 8, 4, 2), ("dp", "space_0", "space_1", "space_2")
    )
    return jax.shard_map(
        on_device,
        mesh=torus,
        in_specs=(
            P("dp", SPACE, None, None),
            P("dp", SPACE, None, None),
            P("dp", SPACE),
            P("dp", SPACE, None),
            P(),
            P(),
            P(),
            P(),
        ),
        out_specs=(P(), P(), P(), P()),
        check_vma=False,
    )
```

```python
import math

import jax
import jax.numpy as jnp
from jax import lax
from jax.sharding import Mesh
from jax.sharding import PartitionSpec as P

SPACE = ("space_0", "space_1", "space_2")


EPS = 1e-05


def from_behind(value, axis, steps):
    count = lax.axis_size(axis)
    first, last = (max(0, -steps), min(count, count - steps))
    return lax.ppermute(value, axis, [(source, source + steps) for source in range(first, last)])


def cut_along(value, dim, peers):
    before, after = (value.shape[:dim], value.shape[dim + 1 :])
    return jnp.moveaxis(value.reshape(*before, peers, -1, *after), dim, 0)


def sent_and_summed(value, axis, dim):
    peers = lax.axis_size(axis)
    pieces = lax.all_to_all(cut_along(value, dim, peers), axis, 0, 0, tiled=True)
    return jnp.sum(pieces, axis=0)


def summed_rows(value, axes, dim):
    far, near = axes
    pieces = cut_along(value, dim, lax.axis_size(far))
    nearer = sent_and_summed(pieces, near, dim + 1)
    arrived = lax.all_to_all(nearer, far, split_axis=0, concat_axis=0, tiled=True)
    return arrived.sum(axis=0)


def rows_for(lines, peers):
    spare = -lines.shape[0] % peers
    if not spare:
        return lines
    return jnp.concatenate([lines, jnp.zeros((spare, *lines.shape[1:]), lines.dtype)])


def from_everyone(value, axis):
    peers = lax.axis_size(axis)
    return lax.all_to_all(
        jnp.broadcast_to(value[None], (peers, *value.shape)), axis, 0, 0, tiled=True
    )


def in_order(pieces, dim):
    pieces = jnp.moveaxis(pieces, 0, dim)
    dims = pieces.shape
    return pieces.reshape(*dims[:dim], dims[dim] * dims[dim + 1], *dims[dim + 2 :])


def gathered_by_axis(value, axes, dim):
    far, near = axes
    first = from_everyone(value, far)
    pieces = jnp.swapaxes(from_everyone(first, near), 0, 1)
    return in_order(pieces.reshape(-1, *value.shape), dim)


def total_of(value, axes):
    lines = value.reshape(-1)
    own = summed_rows(rows_for(lines, lax.axis_size(axes[0]) * lax.axis_size(axes[1])), axes, 0)
    whole = gathered_by_axis(own, axes, 0)
    return whole[: len(lines)].reshape(value.shape)


def norm_forward(values):
    middle = jnp.mean(values, axis=-1, keepdims=True)
    centred = values - middle
    inverse = lax.rsqrt(jnp.mean(centred * centred, axis=-1, keepdims=True) + EPS)
    return (centred * inverse, inverse)


def norm_backward(grad_act, hidden, normed, inverse, gain):
    sig = jax.nn.sigmoid(hidden)
    grad_hidden = grad_act * sig * (1.0 + hidden * (1.0 - sig))
    grad_gain = jnp.sum(grad_hidden * normed, axis=(0, 1, 2))
    scaled = grad_hidden * gain
    centre = jnp.mean(scaled, axis=-1, keepdims=True)
    along = jnp.mean(scaled * normed, axis=-1, keepdims=True)
    return (inverse * (scaled - centre - normed * along), grad_gain)


def select_rows(source, idents, offset):
    positions = jnp.clip(idents - offset, 0, source.shape[0] - 1)
    picked = jnp.take(source, positions, axis=0)
    return jnp.where((idents >= 0)[:, None], picked, jnp.zeros_like(picked))


def select_many(source, requests):
    idents = jnp.concatenate([wanted for wanted, _ in requests])
    shifts = jnp.concatenate([jnp.full(wanted.shape, shift) for wanted, shift in requests])
    picked = select_rows(source, idents, shifts)
    return jnp.split(picked, len(requests))


def assemble(field, south_rows, east_cols, corners):
    lower = jnp.concatenate([field, south_rows[:, None]], axis=1)
    right = jnp.concatenate([east_cols, corners[:, None]], axis=1)
    return jnp.concatenate([lower, right[:, :, None]], axis=2)


def conv_forward(padded, weight):
    return lax.conv_general_dilated(
        padded,
        weight,
        (2, 2),
        "VALID",
        dimension_numbers=("NHWC", "HWIO", "NHWC"),
        preferred_element_type=jnp.float32,
    )


def weight_grad(padded, grad_z):
    return lax.conv_general_dilated(
        padded,
        grad_z,
        (1, 1),
        "VALID",
        rhs_dilation=(2, 2),
        dimension_numbers=("CHWN", "IHWO", "HWNC"),
        preferred_element_type=jnp.float32,
    )


def input_grad(grad_z, weight):
    return lax.conv_general_dilated(
        grad_z,
        weight[::-1, ::-1],
        (1, 1),
        ((2, 2), (2, 2)),
        lhs_dilation=(2, 2),
        dimension_numbers=("NHWC", "HWOI", "NHWC"),
        preferred_element_type=jnp.float32,
    )


def on_device(image, cotangent, live_count, neighbours, weight_one, weight_two, gain_one, gain_two):
    slots = image.shape[1]
    tile = image.shape[2]
    chan_in = weight_one.shape[2]
    chan_mid = weight_one.shape[3]
    chan_out = weight_two.shape[3]
    half = tile // 2
    quarter = tile // 4
    offset = lax.axis_index(SPACE) * slots
    nearby = neighbours[0]
    live = jnp.arange(slots) < live_count[0, 0]
    field = image[0].reshape(slots, tile, tile, chan_in)
    field = jnp.where(live[:, None, None, None], field, jnp.zeros_like(field))
    image_rows = field[:, 0].reshape(slots, tile * chan_in)
    image_cols = field[:, :, 0, :].reshape(slots, tile * chan_in)
    following = from_behind(image_cols, SPACE, -1)
    source = jnp.concatenate([image_rows, image_cols, following], axis=0)
    south_image, east_image, diag_image = select_many(
        source,
        ((nearby[:, 6], offset), (nearby[:, 4], offset - slots), (nearby[:, 7], offset - slots)),
    )
    padded_one = assemble(
        field,
        south_image.reshape(slots, tile, chan_in),
        east_image.reshape(slots, tile, chan_in),
        diag_image[:, :chan_in],
    )
    normed_one, inverse_one = norm_forward(conv_forward(padded_one, weight_one))
    hidden_one = normed_one * gain_one
    act_one = jax.nn.silu(hidden_one).astype(jnp.bfloat16)
    act_rows = act_one[:, 0].reshape(slots, half * chan_mid)
    act_cols = act_one[:, :, 0, :].reshape(slots, half * chan_mid)
    act_following = from_behind(act_cols, SPACE, -1)
    act_source = jnp.concatenate([act_rows, act_cols, act_following], axis=0)
    south_act, east_act, diag_act = select_many(
        act_source,
        ((nearby[:, 6], offset), (nearby[:, 4], offset - slots), (nearby[:, 7], offset - slots)),
    )
    padded_two = assemble(
        act_one,
        south_act.reshape(slots, half, chan_mid),
        east_act.reshape(slots, half, chan_mid),
        diag_act[:, :chan_mid],
    )
    normed_two, inverse_two = norm_forward(conv_forward(padded_two, weight_two))
    hidden_two = normed_two * gain_two
    factor = 1.0 / math.sqrt(lax.axis_size("dp") * lax.axis_size(SPACE) * slots * quarter * quarter)
    grad_out = cotangent[0].reshape(slots, quarter, quarter, chan_out).astype(jnp.float32)
    grad_out = jnp.where(live[:, None, None, None], grad_out * factor, jnp.zeros_like(grad_out))
    grad_z_two, grad_gain_two = norm_backward(
        grad_out, hidden_two, normed_two, inverse_two, gain_two
    )
    grad_z_two = grad_z_two.astype(jnp.bfloat16)
    grad_weight_two = weight_grad(padded_two, grad_z_two)
    grad_padded = input_grad(grad_z_two, weight_two)
    bottom = grad_padded[:, half, :half, :].astype(jnp.bfloat16).reshape(slots, half * chan_mid)
    right = grad_padded[:, :, half, :].astype(jnp.bfloat16).reshape(slots, (half + 1) * chan_mid)
    previous = from_behind(right, SPACE, 1)
    bottom_wide = jnp.concatenate([bottom, jnp.zeros((slots, chan_mid), bottom.dtype)], axis=1)
    rim_source = jnp.concatenate([previous, right, bottom_wide], axis=0)
    from_west, from_diag, from_north = select_many(
        rim_source,
        (
            (nearby[:, 3], offset - slots),
            (nearby[:, 0], offset - slots),
            (nearby[:, 1], offset - 2 * slots),
        ),
    )
    from_west = from_west.reshape(slots, half + 1, chan_mid)
    from_diag = from_diag.reshape(slots, half + 1, chan_mid)
    from_north = from_north[:, : half * chan_mid].reshape(slots, half, chan_mid)
    grad_act = grad_padded[:, :half, :half, :]
    grad_act = grad_act.at[:, 0].add(from_north.astype(jnp.float32))
    grad_act = grad_act.at[:, :, 0].add(from_west[:, :half].astype(jnp.float32))
    grad_act = grad_act.at[:, 0, 0].add(from_diag[:, half].astype(jnp.float32))
    grad_z_one, grad_gain_one = norm_backward(
        grad_act, hidden_one, normed_one, inverse_one, gain_one
    )
    grad_weight_one = weight_grad(padded_one, grad_z_one.astype(jnp.bfloat16))
    parts = (grad_weight_one, grad_weight_two, grad_gain_one, grad_gain_two)
    flat = jnp.concatenate([part.reshape(-1) for part in parts])
    flat = total_of(flat, (("dp", "space_0"), ("space_1", "space_2")))
    sizes = [part.size for part in parts]
    bounds = [sum(sizes[:index]) for index in range(len(sizes) + 1)]
    grad_weight_one, grad_weight_two, grad_gain_one, grad_gain_two = (
        flat[start:end].reshape(part.shape)
        for start, end, part in zip(bounds[:-1], bounds[1:], parts)
    )
    return (grad_weight_one, grad_weight_two, grad_gain_one, grad_gain_two)


def solution(mesh):
    torus = Mesh(
        mesh.devices.reshape(mesh.shape["dp"], 8, 4, 2), ("dp", "space_0", "space_1", "space_2")
    )
    return jax.shard_map(
        on_device,
        mesh=torus,
        in_specs=(
            P("dp", SPACE, None, None),
            P("dp", SPACE, None, None),
            P("dp", SPACE),
            P("dp", SPACE, None),
            P(),
            P(),
            P(),
            P(),
        ),
        out_specs=(P(), P(), P(), P()),
        check_vma=False,
    )
```

```python
import math

import jax
import jax.numpy as jnp
from jax import lax
from jax.sharding import Mesh
from jax.sharding import PartitionSpec as P

SPACE = ("space_0", "space_1", "space_2")


EPS = 1e-05


def from_behind(value, axis, steps):
    count = lax.axis_size(axis)
    first, last = (max(0, -steps), min(count, count - steps))
    return lax.ppermute(value, axis, [(source, source + steps) for source in range(first, last)])


def cut_along(value, dim, peers):
    before, after = (value.shape[:dim], value.shape[dim + 1 :])
    return jnp.moveaxis(value.reshape(*before, peers, -1, *after), dim, 0)


def sent_and_summed(value, axis, dim):
    peers = lax.axis_size(axis)
    pieces = lax.all_to_all(cut_along(value, dim, peers), axis, 0, 0, tiled=True)
    return jnp.sum(pieces, axis=0)


def summed_rows(value, axes, dim):
    far, near = axes
    pieces = cut_along(value, dim, lax.axis_size(far))
    nearer = sent_and_summed(pieces, near, dim + 1)
    arrived = lax.all_to_all(nearer, far, split_axis=0, concat_axis=0, tiled=True)
    return arrived.sum(axis=0)


def rows_for(lines, peers):
    spare = -lines.shape[0] % peers
    if not spare:
        return lines
    return jnp.concatenate([lines, jnp.zeros((spare, *lines.shape[1:]), lines.dtype)])


def from_everyone(value, axis):
    peers = lax.axis_size(axis)
    return lax.all_to_all(
        jnp.broadcast_to(value[None], (peers, *value.shape)), axis, 0, 0, tiled=True
    )


def in_order(pieces, dim):
    pieces = jnp.moveaxis(pieces, 0, dim)
    dims = pieces.shape
    return pieces.reshape(*dims[:dim], dims[dim] * dims[dim + 1], *dims[dim + 2 :])


def gathered_by_axis(value, axes, dim):
    far, near = axes
    first = from_everyone(value, far)
    pieces = jnp.swapaxes(from_everyone(first, near), 0, 1)
    return in_order(pieces.reshape(-1, *value.shape), dim)


def total_of(value, axes):
    lines = value.reshape(-1)
    own = summed_rows(rows_for(lines, lax.axis_size(axes[0]) * lax.axis_size(axes[1])), axes, 0)
    whole = gathered_by_axis(own, axes, 0)
    return whole[: len(lines)].reshape(value.shape)


def summed_everywhere(value, far, near):
    lines = rows_for(value, lax.axis_size(far) * lax.axis_size(near))
    far_peers = lax.axis_size(far)
    mine = lax.all_to_all(lines.reshape(far_peers, -1), far, 0, 0, tiled=True).sum(axis=0)
    mine = from_everyone(mine, near).sum(axis=0)
    return from_everyone(mine, far).reshape(-1)[: value.shape[0]]


def norm_forward(values):
    middle = jnp.mean(values, axis=-1, keepdims=True)
    centred = values - middle
    inverse = lax.rsqrt(jnp.mean(centred * centred, axis=-1, keepdims=True) + EPS)
    return (centred * inverse, inverse)


def norm_backward(grad_act, hidden, normed, inverse, gain):
    sig = jax.nn.sigmoid(hidden)
    grad_hidden = grad_act * sig * (1.0 + hidden * (1.0 - sig))
    grad_gain = jnp.sum(grad_hidden * normed, axis=(0, 1, 2))
    scaled = grad_hidden * gain
    centre = jnp.mean(scaled, axis=-1, keepdims=True)
    along = jnp.mean(scaled * normed, axis=-1, keepdims=True)
    return (inverse * (scaled - centre - normed * along), grad_gain)


def select_rows(source, idents, offset):
    positions = jnp.clip(idents - offset, 0, source.shape[0] - 1)
    picked = jnp.take(source, positions, axis=0)
    return jnp.where((idents >= 0)[:, None], picked, jnp.zeros_like(picked))


def select_many(source, requests):
    idents = jnp.concatenate([wanted for wanted, _ in requests])
    shifts = jnp.concatenate([jnp.full(wanted.shape, shift) for wanted, shift in requests])
    picked = select_rows(source, idents, shifts)
    return jnp.split(picked, len(requests))


def assemble(field, south_rows, east_cols, corners):
    lower = jnp.concatenate([field, south_rows[:, None]], axis=1)
    right = jnp.concatenate([east_cols, corners[:, None]], axis=1)
    return jnp.concatenate([lower, right[:, :, None]], axis=2)


def conv_forward(padded, weight):
    return lax.conv_general_dilated(
        padded,
        weight,
        (2, 2),
        "VALID",
        dimension_numbers=("NHWC", "HWIO", "NHWC"),
        preferred_element_type=jnp.float32,
    )


def weight_grad(padded, grad_z):
    return lax.conv_general_dilated(
        padded,
        grad_z,
        (1, 1),
        "VALID",
        rhs_dilation=(2, 2),
        dimension_numbers=("CHWN", "IHWO", "HWNC"),
        preferred_element_type=jnp.float32,
    )


def input_grad(grad_z, weight):
    return lax.conv_general_dilated(
        grad_z,
        weight[::-1, ::-1],
        (1, 1),
        ((2, 2), (2, 2)),
        lhs_dilation=(2, 2),
        dimension_numbers=("NHWC", "HWOI", "NHWC"),
        preferred_element_type=jnp.float32,
    )


def on_device(image, cotangent, live_count, neighbours, weight_one, weight_two, gain_one, gain_two):
    slots = image.shape[1]
    tile = image.shape[2]
    chan_in = weight_one.shape[2]
    chan_mid = weight_one.shape[3]
    chan_out = weight_two.shape[3]
    half = tile // 2
    quarter = tile // 4
    offset = lax.axis_index(SPACE) * slots
    nearby = neighbours[0]
    live = jnp.arange(slots) < live_count[0, 0]
    field = image[0].reshape(slots, tile, tile, chan_in)
    field = jnp.where(live[:, None, None, None], field, jnp.zeros_like(field))
    image_rows = field[:, 0].reshape(slots, tile * chan_in)
    image_cols = field[:, :, 0, :].reshape(slots, tile * chan_in)
    following = from_behind(image_cols, SPACE, -1)
    source = jnp.concatenate([image_rows, image_cols, following], axis=0)
    south_image, east_image, diag_image = select_many(
        source,
        ((nearby[:, 6], offset), (nearby[:, 4], offset - slots), (nearby[:, 7], offset - slots)),
    )
    padded_one = assemble(
        field,
        south_image.reshape(slots, tile, chan_in),
        east_image.reshape(slots, tile, chan_in),
        diag_image[:, :chan_in],
    )
    normed_one, inverse_one = norm_forward(conv_forward(padded_one, weight_one))
    hidden_one = normed_one * gain_one
    act_one = jax.nn.silu(hidden_one).astype(jnp.bfloat16)
    act_rows = act_one[:, 0].reshape(slots, half * chan_mid)
    act_cols = act_one[:, :, 0, :].reshape(slots, half * chan_mid)
    act_following = from_behind(act_cols, SPACE, -1)
    act_source = jnp.concatenate([act_rows, act_cols, act_following], axis=0)
    south_act, east_act, diag_act = select_many(
        act_source,
        ((nearby[:, 6], offset), (nearby[:, 4], offset - slots), (nearby[:, 7], offset - slots)),
    )
    padded_two = assemble(
        act_one,
        south_act.reshape(slots, half, chan_mid),
        east_act.reshape(slots, half, chan_mid),
        diag_act[:, :chan_mid],
    )
    normed_two, inverse_two = norm_forward(conv_forward(padded_two, weight_two))
    hidden_two = normed_two * gain_two
    factor = 1.0 / math.sqrt(lax.axis_size("dp") * lax.axis_size(SPACE) * slots * quarter * quarter)
    grad_out = cotangent[0].reshape(slots, quarter, quarter, chan_out).astype(jnp.float32)
    grad_out = jnp.where(live[:, None, None, None], grad_out * factor, jnp.zeros_like(grad_out))
    grad_z_two, grad_gain_two = norm_backward(
        grad_out, hidden_two, normed_two, inverse_two, gain_two
    )
    grad_z_two = grad_z_two.astype(jnp.bfloat16)
    grad_weight_two = weight_grad(padded_two, grad_z_two)
    grad_padded = input_grad(grad_z_two, weight_two)
    bottom = grad_padded[:, half, :half, :].astype(jnp.bfloat16).reshape(slots, half * chan_mid)
    right = grad_padded[:, :, half, :].astype(jnp.bfloat16).reshape(slots, (half + 1) * chan_mid)
    previous = from_behind(right, SPACE, 1)
    bottom_wide = jnp.concatenate([bottom, jnp.zeros((slots, chan_mid), bottom.dtype)], axis=1)
    rim_source = jnp.concatenate([previous, right, bottom_wide], axis=0)
    from_west, from_diag, from_north = select_many(
        rim_source,
        (
            (nearby[:, 3], offset - slots),
            (nearby[:, 0], offset - slots),
            (nearby[:, 1], offset - 2 * slots),
        ),
    )
    from_west = from_west.reshape(slots, half + 1, chan_mid)
    from_diag = from_diag.reshape(slots, half + 1, chan_mid)
    from_north = from_north[:, : half * chan_mid].reshape(slots, half, chan_mid)
    grad_act = grad_padded[:, :half, :half, :]
    grad_act = grad_act.at[:, 0].add(from_north.astype(jnp.float32))
    grad_act = grad_act.at[:, :, 0].add(from_west[:, :half].astype(jnp.float32))
    grad_act = grad_act.at[:, 0, 0].add(from_diag[:, half].astype(jnp.float32))
    grad_z_one, grad_gain_one = norm_backward(
        grad_act, hidden_one, normed_one, inverse_one, gain_one
    )
    grad_weight_one = weight_grad(padded_one, grad_z_one.astype(jnp.bfloat16))
    parts = (grad_weight_one, grad_weight_two, grad_gain_one, grad_gain_two)
    flat = jnp.concatenate([part.reshape(-1) for part in parts])
    flat = summed_everywhere(flat, ("dp", "space_0"), ("space_1", "space_2"))
    sizes = [part.size for part in parts]
    bounds = [sum(sizes[:index]) for index in range(len(sizes) + 1)]
    grad_weight_one, grad_weight_two, grad_gain_one, grad_gain_two = (
        flat[start:end].reshape(part.shape)
        for start, end, part in zip(bounds[:-1], bounds[1:], parts)
    )
    return (grad_weight_one, grad_weight_two, grad_gain_one, grad_gain_two)


def solution(mesh):
    torus = Mesh(
        mesh.devices.reshape(mesh.shape["dp"], 8, 4, 2), ("dp", "space_0", "space_1", "space_2")
    )
    return jax.shard_map(
        on_device,
        mesh=torus,
        in_specs=(
            P("dp", SPACE, None, None),
            P("dp", SPACE, None, None),
            P("dp", SPACE),
            P("dp", SPACE, None),
            P(),
            P(),
            P(),
            P(),
        ),
        out_specs=(P(), P(), P(), P()),
        check_vma=False,
    )
```

```python
import math

import jax
import jax.numpy as jnp
from jax import lax
from jax.sharding import Mesh
from jax.sharding import PartitionSpec as P

SPACE = ("space_0", "space_1", "space_2")


EPS = 1e-05


def from_behind(value, axis, steps):
    count = lax.axis_size(axis)
    first, last = (max(0, -steps), min(count, count - steps))
    return lax.ppermute(value, axis, [(source, source + steps) for source in range(first, last)])


def cut_along(value, dim, peers):
    before, after = (value.shape[:dim], value.shape[dim + 1 :])
    return jnp.moveaxis(value.reshape(*before, peers, -1, *after), dim, 0)


def sent_and_summed(value, axis, dim):
    peers = lax.axis_size(axis)
    pieces = lax.all_to_all(cut_along(value, dim, peers), axis, 0, 0, tiled=True)
    return jnp.sum(pieces, axis=0)


def summed_rows(value, axes, dim):
    far, near = axes
    pieces = cut_along(value, dim, lax.axis_size(far))
    nearer = sent_and_summed(pieces, near, dim + 1)
    arrived = lax.all_to_all(nearer, far, split_axis=0, concat_axis=0, tiled=True)
    return arrived.sum(axis=0)


def rows_for(lines, peers):
    spare = -lines.shape[0] % peers
    if not spare:
        return lines
    return jnp.concatenate([lines, jnp.zeros((spare, *lines.shape[1:]), lines.dtype)])


def from_everyone(value, axis):
    peers = lax.axis_size(axis)
    return lax.all_to_all(
        jnp.broadcast_to(value[None], (peers, *value.shape)), axis, 0, 0, tiled=True
    )


def in_order(pieces, dim):
    pieces = jnp.moveaxis(pieces, 0, dim)
    dims = pieces.shape
    return pieces.reshape(*dims[:dim], dims[dim] * dims[dim + 1], *dims[dim + 2 :])


def gathered_by_axis(value, axes, dim):
    far, near = axes
    first = from_everyone(value, far)
    pieces = jnp.swapaxes(from_everyone(first, near), 0, 1)
    return in_order(pieces.reshape(-1, *value.shape), dim)


def total_of(value, axes):
    lines = value.reshape(-1)
    own = summed_rows(rows_for(lines, lax.axis_size(axes[0]) * lax.axis_size(axes[1])), axes, 0)
    whole = gathered_by_axis(own, axes, 0)
    return whole[: len(lines)].reshape(value.shape)


def summed_everywhere(value, far, near):
    lines = rows_for(value, lax.axis_size(far))
    far_peers = lax.axis_size(far)
    pieces = lines.reshape(far_peers, -1, *lines.shape[1:])
    mine = lax.all_to_all(pieces, far, 0, 0, tiled=True).sum(axis=0)
    mine = from_everyone(mine, near).sum(axis=0)
    whole = from_everyone(mine, far)
    return whole.reshape(-1, *value.shape[1:])[: value.shape[0]]


def norm_forward(values):
    middle = jnp.mean(values, axis=-1, keepdims=True)
    centred = values - middle
    inverse = lax.rsqrt(jnp.mean(centred * centred, axis=-1, keepdims=True) + EPS)
    return (centred * inverse, inverse)


def norm_backward(grad_act, hidden, normed, inverse, gain):
    sig = jax.nn.sigmoid(hidden)
    grad_hidden = grad_act * sig * (1.0 + hidden * (1.0 - sig))
    grad_gain = jnp.sum(grad_hidden * normed, axis=(0, 1, 2))
    scaled = grad_hidden * gain
    centre = jnp.mean(scaled, axis=-1, keepdims=True)
    along = jnp.mean(scaled * normed, axis=-1, keepdims=True)
    return (inverse * (scaled - centre - normed * along), grad_gain)


def select_rows(source, idents, offset):
    positions = jnp.clip(idents - offset, 0, source.shape[0] - 1)
    picked = jnp.take(source, positions, axis=0)
    return jnp.where((idents >= 0)[:, None], picked, jnp.zeros_like(picked))


def select_many(source, requests):
    idents = jnp.concatenate([wanted for wanted, _ in requests])
    shifts = jnp.concatenate([jnp.full(wanted.shape, shift) for wanted, shift in requests])
    picked = select_rows(source, idents, shifts)
    return jnp.split(picked, len(requests))


def assemble(field, south_rows, east_cols, corners):
    lower = jnp.concatenate([field, south_rows[:, None]], axis=1)
    right = jnp.concatenate([east_cols, corners[:, None]], axis=1)
    return jnp.concatenate([lower, right[:, :, None]], axis=2)


def conv_forward(padded, weight):
    return lax.conv_general_dilated(
        padded,
        weight,
        (2, 2),
        "VALID",
        dimension_numbers=("NHWC", "HWIO", "NHWC"),
        preferred_element_type=jnp.float32,
    )


def weight_grad(padded, grad_z):
    return lax.conv_general_dilated(
        padded,
        grad_z,
        (1, 1),
        "VALID",
        rhs_dilation=(2, 2),
        dimension_numbers=("CHWN", "IHWO", "HWNC"),
        preferred_element_type=jnp.float32,
    )


def input_grad(grad_z, weight):
    return lax.conv_general_dilated(
        grad_z,
        weight[::-1, ::-1],
        (1, 1),
        ((2, 2), (2, 2)),
        lhs_dilation=(2, 2),
        dimension_numbers=("NHWC", "HWOI", "NHWC"),
        preferred_element_type=jnp.float32,
    )


def on_device(image, cotangent, live_count, neighbours, weight_one, weight_two, gain_one, gain_two):
    slots = image.shape[1]
    tile = image.shape[2]
    chan_in = weight_one.shape[2]
    chan_mid = weight_one.shape[3]
    chan_out = weight_two.shape[3]
    half = tile // 2
    quarter = tile // 4
    offset = lax.axis_index(SPACE) * slots
    nearby = neighbours[0]
    live = jnp.arange(slots) < live_count[0, 0]
    field = image[0].reshape(slots, tile, tile, chan_in)
    field = jnp.where(live[:, None, None, None], field, jnp.zeros_like(field))
    image_rows = field[:, 0].reshape(slots, tile * chan_in)
    image_cols = field[:, :, 0, :].reshape(slots, tile * chan_in)
    following = from_behind(image_cols, SPACE, -1)
    source = jnp.concatenate([image_rows, image_cols, following], axis=0)
    south_image, east_image, diag_image = select_many(
        source,
        ((nearby[:, 6], offset), (nearby[:, 4], offset - slots), (nearby[:, 7], offset - slots)),
    )
    padded_one = assemble(
        field,
        south_image.reshape(slots, tile, chan_in),
        east_image.reshape(slots, tile, chan_in),
        diag_image[:, :chan_in],
    )
    normed_one, inverse_one = norm_forward(conv_forward(padded_one, weight_one))
    hidden_one = normed_one * gain_one
    act_one = jax.nn.silu(hidden_one).astype(jnp.bfloat16)
    act_rows = act_one[:, 0].reshape(slots, half * chan_mid)
    act_cols = act_one[:, :, 0, :].reshape(slots, half * chan_mid)
    act_following = from_behind(act_cols, SPACE, -1)
    act_source = jnp.concatenate([act_rows, act_cols, act_following], axis=0)
    south_act, east_act, diag_act = select_many(
        act_source,
        ((nearby[:, 6], offset), (nearby[:, 4], offset - slots), (nearby[:, 7], offset - slots)),
    )
    padded_two = assemble(
        act_one,
        south_act.reshape(slots, half, chan_mid),
        east_act.reshape(slots, half, chan_mid),
        diag_act[:, :chan_mid],
    )
    normed_two, inverse_two = norm_forward(conv_forward(padded_two, weight_two))
    hidden_two = normed_two * gain_two
    factor = 1.0 / math.sqrt(lax.axis_size("dp") * lax.axis_size(SPACE) * slots * quarter * quarter)
    grad_out = cotangent[0].reshape(slots, quarter, quarter, chan_out).astype(jnp.float32)
    grad_out = jnp.where(live[:, None, None, None], grad_out * factor, jnp.zeros_like(grad_out))
    grad_z_two, grad_gain_two = norm_backward(
        grad_out, hidden_two, normed_two, inverse_two, gain_two
    )
    grad_z_two = grad_z_two.astype(jnp.bfloat16)
    grad_weight_two = weight_grad(padded_two, grad_z_two)
    grad_padded = input_grad(grad_z_two, weight_two)
    bottom = grad_padded[:, half, :half, :].astype(jnp.bfloat16).reshape(slots, half * chan_mid)
    right = grad_padded[:, :, half, :].astype(jnp.bfloat16).reshape(slots, (half + 1) * chan_mid)
    previous = from_behind(right, SPACE, 1)
    bottom_wide = jnp.concatenate([bottom, jnp.zeros((slots, chan_mid), bottom.dtype)], axis=1)
    rim_source = jnp.concatenate([previous, right, bottom_wide], axis=0)
    from_west, from_diag, from_north = select_many(
        rim_source,
        (
            (nearby[:, 3], offset - slots),
            (nearby[:, 0], offset - slots),
            (nearby[:, 1], offset - 2 * slots),
        ),
    )
    from_west = from_west.reshape(slots, half + 1, chan_mid)
    from_diag = from_diag.reshape(slots, half + 1, chan_mid)
    from_north = from_north[:, : half * chan_mid].reshape(slots, half, chan_mid)
    grad_act = grad_padded[:, :half, :half, :]
    grad_act = grad_act.at[:, 0].add(from_north.astype(jnp.float32))
    grad_act = grad_act.at[:, :, 0].add(from_west[:, :half].astype(jnp.float32))
    grad_act = grad_act.at[:, 0, 0].add(from_diag[:, half].astype(jnp.float32))
    grad_z_one, grad_gain_one = norm_backward(
        grad_act, hidden_one, normed_one, inverse_one, gain_one
    )
    grad_weight_one = weight_grad(padded_one, grad_z_one.astype(jnp.bfloat16))
    parts = (grad_weight_one, grad_weight_two, grad_gain_one, grad_gain_two)
    rows = jnp.concatenate([part.reshape(-1, chan_mid) for part in parts])
    rows = summed_everywhere(rows, ("dp", "space_0"), ("space_1", "space_2"))
    sizes = [part.size // chan_mid for part in parts]
    bounds = [sum(sizes[:index]) for index in range(len(sizes) + 1)]
    grad_weight_one, grad_weight_two, grad_gain_one, grad_gain_two = (
        rows[start:end].reshape(part.shape)
        for start, end, part in zip(bounds[:-1], bounds[1:], parts)
    )
    return (grad_weight_one, grad_weight_two, grad_gain_one, grad_gain_two)


def solution(mesh):
    torus = Mesh(
        mesh.devices.reshape(mesh.shape["dp"], 8, 4, 2), ("dp", "space_0", "space_1", "space_2")
    )
    return jax.shard_map(
        on_device,
        mesh=torus,
        in_specs=(
            P("dp", SPACE, None, None),
            P("dp", SPACE, None, None),
            P("dp", SPACE),
            P("dp", SPACE, None),
            P(),
            P(),
            P(),
            P(),
        ),
        out_specs=(P(), P(), P(), P()),
        check_vma=False,
    )
```

```python
import math

import jax
import jax.numpy as jnp
from jax import lax
from jax.sharding import Mesh
from jax.sharding import PartitionSpec as P

SPACE = ("space_0", "space_1", "space_2")


EPS = 1e-05


def from_behind(value, axis, steps):
    count = lax.axis_size(axis)
    first, last = (max(0, -steps), min(count, count - steps))
    return lax.ppermute(value, axis, [(source, source + steps) for source in range(first, last)])


def cut_along(value, dim, peers):
    before, after = (value.shape[:dim], value.shape[dim + 1 :])
    return jnp.moveaxis(value.reshape(*before, peers, -1, *after), dim, 0)


def sent_and_summed(value, axis, dim):
    peers = lax.axis_size(axis)
    pieces = lax.all_to_all(cut_along(value, dim, peers), axis, 0, 0, tiled=True)
    return jnp.sum(pieces, axis=0)


def summed_rows(value, axes, dim):
    far, near = axes
    pieces = cut_along(value, dim, lax.axis_size(far))
    nearer = sent_and_summed(pieces, near, dim + 1)
    arrived = lax.all_to_all(nearer, far, split_axis=0, concat_axis=0, tiled=True)
    return arrived.sum(axis=0)


def rows_for(lines, peers):
    spare = -lines.shape[0] % peers
    if not spare:
        return lines
    return jnp.concatenate([lines, jnp.zeros((spare, *lines.shape[1:]), lines.dtype)])


def from_everyone(value, axis):
    peers = lax.axis_size(axis)
    return lax.all_to_all(
        jnp.broadcast_to(value[None], (peers, *value.shape)), axis, 0, 0, tiled=True
    )


def in_order(pieces, dim):
    pieces = jnp.moveaxis(pieces, 0, dim)
    dims = pieces.shape
    return pieces.reshape(*dims[:dim], dims[dim] * dims[dim + 1], *dims[dim + 2 :])


def gathered_by_axis(value, axes, dim):
    far, near = axes
    first = from_everyone(value, far)
    pieces = jnp.swapaxes(from_everyone(first, near), 0, 1)
    return in_order(pieces.reshape(-1, *value.shape), dim)


def total_of(value, axes):
    lines = value.reshape(-1)
    own = summed_rows(rows_for(lines, lax.axis_size(axes[0]) * lax.axis_size(axes[1])), axes, 0)
    whole = gathered_by_axis(own, axes, 0)
    return whole[: len(lines)].reshape(value.shape)


def summed_everywhere(value, far, near):
    lines = rows_for(value, lax.axis_size(far) * lax.axis_size(near))
    far_peers = lax.axis_size(far)
    mine = lax.all_to_all(lines.reshape(far_peers, -1), far, 0, 0, tiled=True).sum(axis=0)
    mine = from_everyone(mine, near).sum(axis=0)
    return from_everyone(mine, far).reshape(-1)[: value.shape[0]]


def norm_forward(values):
    middle = jnp.mean(values, axis=-1, keepdims=True)
    centred = values - middle
    inverse = lax.rsqrt(jnp.mean(centred * centred, axis=-1, keepdims=True) + EPS)
    return (centred * inverse, inverse)


def norm_backward(grad_act, hidden, normed, inverse, gain):
    sig = jax.nn.sigmoid(hidden)
    grad_hidden = grad_act * sig * (1.0 + hidden * (1.0 - sig))
    grad_gain = jnp.sum(grad_hidden * normed, axis=(0, 1, 2))
    scaled = grad_hidden * gain
    centre = jnp.mean(scaled, axis=-1, keepdims=True)
    along = jnp.mean(scaled * normed, axis=-1, keepdims=True)
    return (inverse * (scaled - centre - normed * along), grad_gain)


def select_rows(source, idents, offset):
    positions = jnp.clip(idents - offset, 0, source.shape[0] - 1)
    picked = jnp.take(source, positions, axis=0)
    return jnp.where((idents >= 0)[:, None], picked, jnp.zeros_like(picked))


def select_many(source, requests):
    idents = jnp.concatenate([wanted for wanted, _ in requests])
    shifts = jnp.concatenate([jnp.full(wanted.shape, shift) for wanted, shift in requests])
    picked = select_rows(source, idents, shifts)
    return jnp.split(picked, len(requests))


def assemble(field, south_rows, east_cols, corners):
    lower = jnp.concatenate([field, south_rows[:, None]], axis=1)
    right = jnp.concatenate([east_cols, corners[:, None]], axis=1)
    return jnp.concatenate([lower, right[:, :, None]], axis=2)


def conv_forward(padded, weight):
    return lax.conv_general_dilated(
        padded,
        weight,
        (2, 2),
        "VALID",
        dimension_numbers=("NHWC", "HWIO", "NHWC"),
        preferred_element_type=jnp.float32,
    )


def weight_grad(padded, grad_z):
    return lax.conv_general_dilated(
        padded,
        grad_z,
        (1, 1),
        "VALID",
        rhs_dilation=(2, 2),
        dimension_numbers=("CHWN", "IHWO", "HWNC"),
        preferred_element_type=jnp.float32,
    )


def input_grad(grad_z, weight):
    return lax.conv_general_dilated(
        grad_z,
        weight[::-1, ::-1],
        (1, 1),
        ((2, 2), (2, 2)),
        lhs_dilation=(2, 2),
        dimension_numbers=("NHWC", "HWOI", "NHWC"),
        preferred_element_type=jnp.float32,
    )


def on_device(image, cotangent, live_count, neighbours, weight_one, weight_two, gain_one, gain_two):
    slots = image.shape[1]
    tile = image.shape[2]
    chan_in = weight_one.shape[2]
    chan_mid = weight_one.shape[3]
    chan_out = weight_two.shape[3]
    half = tile // 2
    quarter = tile // 4
    offset = lax.axis_index(SPACE) * slots
    nearby = neighbours[0]
    live = jnp.arange(slots) < live_count[0, 0]
    field = image[0].reshape(slots, tile, tile, chan_in)
    field = jnp.where(live[:, None, None, None], field, jnp.zeros_like(field))
    image_rows = field[:, 0].reshape(slots, tile * chan_in)
    south_image = select_rows(image_rows, nearby[:, 6], offset).reshape(slots, 1, tile, chan_in)
    strip = jnp.concatenate([field, south_image], axis=1)[:, :, :3, :]
    strip_following = from_behind(strip, SPACE, -1)
    image_cols = field[:, :, 0, :].reshape(slots, tile * chan_in)
    following = strip_following[:, :tile, 0, :].reshape(slots, tile * chan_in)
    source = jnp.concatenate([image_cols, following], axis=0)
    east_image, diag_image = select_many(
        source, ((nearby[:, 4], offset), (nearby[:, 7], offset))
    )
    padded_one = assemble(
        field,
        south_image[:, 0],
        east_image.reshape(slots, tile, chan_in),
        diag_image[:, :chan_in],
    )
    normed_one, inverse_one = norm_forward(conv_forward(padded_one, weight_one))
    hidden_one = normed_one * gain_one
    act_one = jax.nn.silu(hidden_one).astype(jnp.bfloat16)
    normed_edge, _ = norm_forward(conv_forward(strip_following, weight_one))
    act_following = jax.nn.silu(normed_edge * gain_one).astype(jnp.bfloat16)
    act_following = act_following.reshape(slots, half * chan_mid)
    act_rows = act_one[:, 0].reshape(slots, half * chan_mid)
    act_cols = act_one[:, :, 0, :].reshape(slots, half * chan_mid)
    act_source = jnp.concatenate([act_rows, act_cols, act_following], axis=0)
    south_act, east_act, diag_act = select_many(
        act_source,
        ((nearby[:, 6], offset), (nearby[:, 4], offset - slots), (nearby[:, 7], offset - slots)),
    )
    padded_two = assemble(
        act_one,
        south_act.reshape(slots, half, chan_mid),
        east_act.reshape(slots, half, chan_mid),
        diag_act[:, :chan_mid],
    )
    normed_two, inverse_two = norm_forward(conv_forward(padded_two, weight_two))
    hidden_two = normed_two * gain_two
    factor = 1.0 / math.sqrt(lax.axis_size("dp") * lax.axis_size(SPACE) * slots * quarter * quarter)
    grad_out = cotangent[0].reshape(slots, quarter, quarter, chan_out).astype(jnp.float32)
    grad_out = jnp.where(live[:, None, None, None], grad_out * factor, jnp.zeros_like(grad_out))
    grad_z_two, grad_gain_two = norm_backward(
        grad_out, hidden_two, normed_two, inverse_two, gain_two
    )
    grad_z_two = grad_z_two.astype(jnp.bfloat16)
    grad_weight_two = weight_grad(padded_two, grad_z_two)
    grad_padded = input_grad(grad_z_two, weight_two)
    bottom = grad_padded[:, half, :half, :].astype(jnp.bfloat16).reshape(slots, half * chan_mid)
    right = grad_padded[:, :, half, :].astype(jnp.bfloat16).reshape(slots, (half + 1) * chan_mid)
    previous = from_behind(right, SPACE, 1)
    bottom_wide = jnp.concatenate([bottom, jnp.zeros((slots, chan_mid), bottom.dtype)], axis=1)
    rim_source = jnp.concatenate([previous, right, bottom_wide], axis=0)
    from_west, from_diag, from_north = select_many(
        rim_source,
        (
            (nearby[:, 3], offset - slots),
            (nearby[:, 0], offset - slots),
            (nearby[:, 1], offset - 2 * slots),
        ),
    )
    from_west = from_west.reshape(slots, half + 1, chan_mid)
    from_diag = from_diag.reshape(slots, half + 1, chan_mid)
    from_north = from_north[:, : half * chan_mid].reshape(slots, half, chan_mid)
    grad_act = grad_padded[:, :half, :half, :]
    grad_act = grad_act.at[:, 0].add(from_north.astype(jnp.float32))
    grad_act = grad_act.at[:, :, 0].add(from_west[:, :half].astype(jnp.float32))
    grad_act = grad_act.at[:, 0, 0].add(from_diag[:, half].astype(jnp.float32))
    grad_z_one, grad_gain_one = norm_backward(
        grad_act, hidden_one, normed_one, inverse_one, gain_one
    )
    grad_weight_one = weight_grad(padded_one, grad_z_one.astype(jnp.bfloat16))
    parts = (grad_weight_one, grad_weight_two, grad_gain_one, grad_gain_two)
    flat = jnp.concatenate([part.reshape(-1) for part in parts])
    flat = summed_everywhere(flat, ("dp", "space_0"), ("space_1", "space_2"))
    sizes = [part.size for part in parts]
    bounds = [sum(sizes[:index]) for index in range(len(sizes) + 1)]
    grad_weight_one, grad_weight_two, grad_gain_one, grad_gain_two = (
        flat[start:end].reshape(part.shape)
        for start, end, part in zip(bounds[:-1], bounds[1:], parts)
    )
    return (grad_weight_one, grad_weight_two, grad_gain_one, grad_gain_two)


def solution(mesh):
    torus = Mesh(
        mesh.devices.reshape(mesh.shape["dp"], 8, 4, 2), ("dp", "space_0", "space_1", "space_2")
    )
    return jax.shard_map(
        on_device,
        mesh=torus,
        in_specs=(
            P("dp", SPACE, None, None),
            P("dp", SPACE, None, None),
            P("dp", SPACE),
            P("dp", SPACE, None),
            P(),
            P(),
            P(),
            P(),
        ),
        out_specs=(P(), P(), P(), P()),
        check_vma=False,
    )
```

```python
import math

import jax
import jax.numpy as jnp
from jax import lax
from jax.sharding import Mesh
from jax.sharding import PartitionSpec as P

SPACE = ("space_0", "space_1", "space_2")


EPS = 1e-05


def from_behind(value, axis, steps):
    count = lax.axis_size(axis)
    first, last = (max(0, -steps), min(count, count - steps))
    return lax.ppermute(value, axis, [(source, source + steps) for source in range(first, last)])


def cut_along(value, dim, peers):
    before, after = (value.shape[:dim], value.shape[dim + 1 :])
    return jnp.moveaxis(value.reshape(*before, peers, -1, *after), dim, 0)


def sent_and_summed(value, axis, dim):
    peers = lax.axis_size(axis)
    pieces = lax.all_to_all(cut_along(value, dim, peers), axis, 0, 0, tiled=True)
    return jnp.sum(pieces, axis=0)


def summed_rows(value, axes, dim):
    far, near = axes
    pieces = cut_along(value, dim, lax.axis_size(far))
    nearer = sent_and_summed(pieces, near, dim + 1)
    arrived = lax.all_to_all(nearer, far, split_axis=0, concat_axis=0, tiled=True)
    return arrived.sum(axis=0)


def rows_for(lines, peers):
    spare = -lines.shape[0] % peers
    if not spare:
        return lines
    return jnp.concatenate([lines, jnp.zeros((spare, *lines.shape[1:]), lines.dtype)])


def from_everyone(value, axis):
    peers = lax.axis_size(axis)
    return lax.all_to_all(
        jnp.broadcast_to(value[None], (peers, *value.shape)), axis, 0, 0, tiled=True
    )


def in_order(pieces, dim):
    pieces = jnp.moveaxis(pieces, 0, dim)
    dims = pieces.shape
    return pieces.reshape(*dims[:dim], dims[dim] * dims[dim + 1], *dims[dim + 2 :])


def gathered_by_axis(value, axes, dim):
    far, near = axes
    first = from_everyone(value, far)
    pieces = jnp.swapaxes(from_everyone(first, near), 0, 1)
    return in_order(pieces.reshape(-1, *value.shape), dim)


def total_of(value, axes):
    lines = value.reshape(-1)
    own = summed_rows(rows_for(lines, lax.axis_size(axes[0]) * lax.axis_size(axes[1])), axes, 0)
    whole = gathered_by_axis(own, axes, 0)
    return whole[: len(lines)].reshape(value.shape)


def summed_everywhere(value, far, near):
    lines = rows_for(value, lax.axis_size(far) * lax.axis_size(near))
    far_peers = lax.axis_size(far)
    mine = lax.all_to_all(lines.reshape(far_peers, -1), far, 0, 0, tiled=True).sum(axis=0)
    mine = from_everyone(mine, near).sum(axis=0)
    return from_everyone(mine, far).reshape(-1)[: value.shape[0]]


def norm_forward(values):
    middle = jnp.mean(values, axis=-1, keepdims=True)
    centred = values - middle
    inverse = lax.rsqrt(jnp.mean(centred * centred, axis=-1, keepdims=True) + EPS)
    return (centred * inverse, inverse)


def norm_backward(grad_act, hidden, normed, inverse, gain):
    sig = jax.nn.sigmoid(hidden)
    grad_hidden = grad_act * sig * (1.0 + hidden * (1.0 - sig))
    grad_gain = jnp.sum(grad_hidden * normed, axis=(0, 1, 2))
    scaled = grad_hidden * gain
    centre = jnp.mean(scaled, axis=-1, keepdims=True)
    along = jnp.mean(scaled * normed, axis=-1, keepdims=True)
    return (inverse * (scaled - centre - normed * along), grad_gain)


def select_rows(source, idents, offset):
    positions = jnp.clip(idents - offset, 0, source.shape[0] - 1)
    picked = jnp.take(source, positions, axis=0)
    return jnp.where((idents >= 0)[:, None], picked, jnp.zeros_like(picked))


def select_many(source, requests):
    idents = jnp.concatenate([wanted for wanted, _ in requests])
    shifts = jnp.concatenate([jnp.full(wanted.shape, shift) for wanted, shift in requests])
    picked = select_rows(source, idents, shifts)
    return jnp.split(picked, len(requests))


def assemble(field, south_rows, east_cols, corners):
    lower = jnp.concatenate([field, south_rows[:, None]], axis=1)
    right = jnp.concatenate([east_cols, corners[:, None]], axis=1)
    return jnp.concatenate([lower, right[:, :, None]], axis=2)


def conv_forward(padded, weight):
    return lax.conv_general_dilated(
        padded,
        weight,
        (2, 2),
        "VALID",
        dimension_numbers=("NHWC", "HWIO", "NHWC"),
        preferred_element_type=jnp.float32,
    )


def weight_grad(padded, grad_z):
    return lax.conv_general_dilated(
        padded,
        grad_z,
        (1, 1),
        "VALID",
        rhs_dilation=(2, 2),
        dimension_numbers=("CHWN", "IHWO", "HWNC"),
        preferred_element_type=jnp.float32,
    )


def input_grad(grad_z, weight):
    return lax.conv_general_dilated(
        grad_z,
        weight[::-1, ::-1],
        (1, 1),
        ((2, 2), (2, 2)),
        lhs_dilation=(2, 2),
        dimension_numbers=("NHWC", "HWOI", "NHWC"),
        preferred_element_type=jnp.float32,
    )


def on_device(image, cotangent, live_count, neighbours, weight_one, weight_two, gain_one, gain_two):
    slots = image.shape[1]
    tile = image.shape[2]
    chan_in = weight_one.shape[2]
    chan_mid = weight_one.shape[3]
    chan_out = weight_two.shape[3]
    half = tile // 2
    quarter = tile // 4
    offset = lax.axis_index(SPACE) * slots
    nearby = neighbours[0]
    live = jnp.arange(slots) < live_count[0, 0]
    raw = image[0].reshape(slots, tile, tile, chan_in)
    edge = raw[:, :, :3, :].reshape(slots, tile * 3 * chan_in)
    edge_following = from_behind(edge, SPACE, -1)
    field = jnp.where(live[:, None, None, None], raw, jnp.zeros_like(raw))
    pool = jnp.concatenate([edge, edge_following], axis=0)
    east_strip, diag_strip = select_many(pool, ((nearby[:, 4], offset), (nearby[:, 7], offset)))
    east_strip = east_strip.reshape(slots, tile, 3, chan_in)
    diag_strip = diag_strip.reshape(slots, tile, 3, chan_in)
    south_image = select_rows(field[:, 0].reshape(slots, tile * chan_in), nearby[:, 6], offset)
    padded_one = assemble(
        field,
        south_image.reshape(slots, tile, chan_in),
        east_strip[:, :, 0, :],
        diag_strip[:, 0, 0, :],
    )

    def activation(padded):
        normed, inverse = norm_forward(conv_forward(padded, weight_one))
        hidden = normed * gain_one
        return normed, inverse, hidden, jax.nn.silu(hidden).astype(jnp.bfloat16)

    normed_one, inverse_one, hidden_one, act_one = activation(padded_one)
    east_act = activation(jnp.concatenate([east_strip, diag_strip[:, :1]], axis=1))[3]
    east_act = jnp.where((nearby[:, 4] >= 0)[:, None, None, None], east_act, jnp.zeros_like(east_act))
    diag_act = activation(diag_strip[:, :3])[3]
    south_act = select_rows(act_one[:, 0].reshape(slots, half * chan_mid), nearby[:, 6], offset)
    padded_two = assemble(
        act_one,
        south_act.reshape(slots, half, chan_mid),
        east_act.reshape(slots, half, chan_mid),
        diag_act.reshape(slots, chan_mid),
    )
    normed_two, inverse_two = norm_forward(conv_forward(padded_two, weight_two))
    hidden_two = normed_two * gain_two
    factor = 1.0 / math.sqrt(lax.axis_size("dp") * lax.axis_size(SPACE) * slots * quarter * quarter)
    grad_out = cotangent[0].reshape(slots, quarter, quarter, chan_out).astype(jnp.float32)
    grad_out = jnp.where(live[:, None, None, None], grad_out * factor, jnp.zeros_like(grad_out))
    grad_z_two, grad_gain_two = norm_backward(
        grad_out, hidden_two, normed_two, inverse_two, gain_two
    )
    grad_z_two = grad_z_two.astype(jnp.bfloat16)
    grad_weight_two = weight_grad(padded_two, grad_z_two)
    grad_padded = input_grad(grad_z_two, weight_two)
    bottom = grad_padded[:, half, :half, :].astype(jnp.bfloat16).reshape(slots, half * chan_mid)
    right = grad_padded[:, :, half, :].astype(jnp.bfloat16).reshape(slots, (half + 1) * chan_mid)
    previous = from_behind(right, SPACE, 1)
    bottom_wide = jnp.concatenate([bottom, jnp.zeros((slots, chan_mid), bottom.dtype)], axis=1)
    rim_source = jnp.concatenate([previous, right, bottom_wide], axis=0)
    from_west, from_diag, from_north = select_many(
        rim_source,
        (
            (nearby[:, 3], offset - slots),
            (nearby[:, 0], offset - slots),
            (nearby[:, 1], offset - 2 * slots),
        ),
    )
    from_west = from_west.reshape(slots, half + 1, chan_mid)
    from_diag = from_diag.reshape(slots, half + 1, chan_mid)
    from_north = from_north[:, : half * chan_mid].reshape(slots, half, chan_mid)
    grad_act = grad_padded[:, :half, :half, :]
    grad_act = grad_act.at[:, 0].add(from_north.astype(jnp.float32))
    grad_act = grad_act.at[:, :, 0].add(from_west[:, :half].astype(jnp.float32))
    grad_act = grad_act.at[:, 0, 0].add(from_diag[:, half].astype(jnp.float32))
    grad_z_one, grad_gain_one = norm_backward(
        grad_act, hidden_one, normed_one, inverse_one, gain_one
    )
    grad_weight_one = weight_grad(padded_one, grad_z_one.astype(jnp.bfloat16))
    parts = (grad_weight_one, grad_weight_two, grad_gain_one, grad_gain_two)
    flat = jnp.concatenate([part.reshape(-1) for part in parts])
    flat = summed_everywhere(flat, ("dp", "space_0"), ("space_1", "space_2"))
    sizes = [part.size for part in parts]
    bounds = [sum(sizes[:index]) for index in range(len(sizes) + 1)]
    grad_weight_one, grad_weight_two, grad_gain_one, grad_gain_two = (
        flat[start:end].reshape(part.shape)
        for start, end, part in zip(bounds[:-1], bounds[1:], parts)
    )
    return (grad_weight_one, grad_weight_two, grad_gain_one, grad_gain_two)


def solution(mesh):
    torus = Mesh(
        mesh.devices.reshape(mesh.shape["dp"], 8, 4, 2), ("dp", "space_0", "space_1", "space_2")
    )
    return jax.shard_map(
        on_device,
        mesh=torus,
        in_specs=(
            P("dp", SPACE, None, None),
            P("dp", SPACE, None, None),
            P("dp", SPACE),
            P("dp", SPACE, None),
            P(),
            P(),
            P(),
            P(),
        ),
        out_specs=(P(), P(), P(), P()),
        check_vma=False,
    )
```

```python
import math

import jax
import jax.numpy as jnp
from jax import lax
from jax.sharding import Mesh
from jax.sharding import PartitionSpec as P

SPACE = ("space_0", "space_1", "space_2")


EPS = 1e-05


def from_behind(value, axis, steps):
    count = lax.axis_size(axis)
    first, last = (max(0, -steps), min(count, count - steps))
    return lax.ppermute(value, axis, [(source, source + steps) for source in range(first, last)])


def cut_along(value, dim, peers):
    before, after = (value.shape[:dim], value.shape[dim + 1 :])
    return jnp.moveaxis(value.reshape(*before, peers, -1, *after), dim, 0)


def sent_and_summed(value, axis, dim):
    peers = lax.axis_size(axis)
    pieces = lax.all_to_all(cut_along(value, dim, peers), axis, 0, 0, tiled=True)
    return jnp.sum(pieces, axis=0)


def summed_rows(value, axes, dim):
    far, near = axes
    pieces = cut_along(value, dim, lax.axis_size(far))
    nearer = sent_and_summed(pieces, near, dim + 1)
    arrived = lax.all_to_all(nearer, far, split_axis=0, concat_axis=0, tiled=True)
    return arrived.sum(axis=0)


def rows_for(lines, peers):
    spare = -lines.shape[0] % peers
    if not spare:
        return lines
    return jnp.concatenate([lines, jnp.zeros((spare, *lines.shape[1:]), lines.dtype)])


def from_everyone(value, axis):
    peers = lax.axis_size(axis)
    return lax.all_to_all(
        jnp.broadcast_to(value[None], (peers, *value.shape)), axis, 0, 0, tiled=True
    )


def in_order(pieces, dim):
    pieces = jnp.moveaxis(pieces, 0, dim)
    dims = pieces.shape
    return pieces.reshape(*dims[:dim], dims[dim] * dims[dim + 1], *dims[dim + 2 :])


def gathered_by_axis(value, axes, dim):
    far, near = axes
    first = from_everyone(value, far)
    pieces = jnp.swapaxes(from_everyone(first, near), 0, 1)
    return in_order(pieces.reshape(-1, *value.shape), dim)


def total_of(value, axes):
    lines = value.reshape(-1)
    own = summed_rows(rows_for(lines, lax.axis_size(axes[0]) * lax.axis_size(axes[1])), axes, 0)
    whole = gathered_by_axis(own, axes, 0)
    return whole[: len(lines)].reshape(value.shape)


def summed_everywhere(value, far, near):
    lines = rows_for(value, lax.axis_size(far) * lax.axis_size(near))
    far_peers = lax.axis_size(far)
    mine = lax.all_to_all(lines.reshape(far_peers, -1), far, 0, 0, tiled=True).sum(axis=0)
    mine = from_everyone(mine, near).sum(axis=0)
    return from_everyone(mine, far).reshape(-1)[: value.shape[0]]


def norm_forward(values):
    middle = jnp.mean(values, axis=-1, keepdims=True)
    centred = values - middle
    inverse = lax.rsqrt(jnp.mean(centred * centred, axis=-1, keepdims=True) + EPS)
    return (centred * inverse, inverse)


def norm_backward(grad_act, hidden, normed, inverse, gain):
    sig = jax.nn.sigmoid(hidden)
    grad_hidden = grad_act * sig * (1.0 + hidden * (1.0 - sig))
    grad_gain = jnp.sum(grad_hidden * normed, axis=(0, 1, 2))
    scaled = grad_hidden * gain
    centre = jnp.mean(scaled, axis=-1, keepdims=True)
    along = jnp.mean(scaled * normed, axis=-1, keepdims=True)
    return (inverse * (scaled - centre - normed * along), grad_gain)


def select_rows(source, idents, offset):
    positions = jnp.clip(idents - offset, 0, source.shape[0] - 1)
    picked = jnp.take(source, positions, axis=0)
    return jnp.where((idents >= 0)[:, None], picked, jnp.zeros_like(picked))


def select_many(source, requests):
    idents = jnp.concatenate([wanted for wanted, _ in requests])
    shifts = jnp.concatenate([jnp.full(wanted.shape, shift) for wanted, shift in requests])
    picked = select_rows(source, idents, shifts)
    return jnp.split(picked, len(requests))


def assemble(field, south_rows, east_cols, corners):
    lower = jnp.concatenate([field, south_rows[:, None]], axis=1)
    right = jnp.concatenate([east_cols, corners[:, None]], axis=1)
    return jnp.concatenate([lower, right[:, :, None]], axis=2)


def conv_forward(padded, weight):
    return lax.conv_general_dilated(
        padded,
        weight,
        (2, 2),
        "VALID",
        dimension_numbers=("NHWC", "HWIO", "NHWC"),
        preferred_element_type=jnp.float32,
    )


def weight_grad(padded, grad_z):
    return lax.conv_general_dilated(
        padded,
        grad_z,
        (1, 1),
        "VALID",
        rhs_dilation=(2, 2),
        dimension_numbers=("CHWN", "IHWO", "HWNC"),
        preferred_element_type=jnp.float32,
    )


def input_grad(grad_z, weight):
    return lax.conv_general_dilated(
        grad_z,
        weight[::-1, ::-1],
        (1, 1),
        ((2, 2), (2, 2)),
        lhs_dilation=(2, 2),
        dimension_numbers=("NHWC", "HWOI", "NHWC"),
        preferred_element_type=jnp.float32,
    )


def on_device(image, cotangent, live_count, neighbours, weight_one, weight_two, gain_one, gain_two):
    slots = image.shape[1]
    tile = image.shape[2]
    chan_in = weight_one.shape[2]
    chan_mid = weight_one.shape[3]
    chan_out = weight_two.shape[3]
    half = tile // 2
    quarter = tile // 4
    offset = lax.axis_index(SPACE) * slots
    nearby = neighbours[0]
    live = jnp.arange(slots) < live_count[0, 0]
    field = image[0].reshape(slots, tile, tile, chan_in)
    field = jnp.where(live[:, None, None, None], field, jnp.zeros_like(field))
    image_rows = field[:, 0].reshape(slots, tile * chan_in)
    south_image = select_rows(image_rows, nearby[:, 6], offset).reshape(slots, 1, tile, chan_in)
    strip = jnp.concatenate([field, south_image], axis=1)[:, :, :3, :]
    strip_following = from_behind(strip, SPACE, -1)
    image_cols = field[:, :, 0, :].reshape(slots, tile * chan_in)
    following = strip_following[:, :tile, 0, :].reshape(slots, tile * chan_in)
    source = jnp.concatenate([image_cols, following], axis=0)
    east_image, diag_image = select_many(
        source, ((nearby[:, 4], offset), (nearby[:, 7], offset))
    )
    padded_one = assemble(
        field,
        south_image[:, 0],
        east_image.reshape(slots, tile, chan_in),
        diag_image[:, :chan_in],
    )
    normed_one, inverse_one = norm_forward(conv_forward(padded_one, weight_one))
    hidden_one = normed_one * gain_one
    act_one = jax.nn.silu(hidden_one).astype(jnp.bfloat16)
    normed_edge, _ = norm_forward(conv_forward(strip_following, weight_one))
    act_following = jax.nn.silu(normed_edge * gain_one).astype(jnp.bfloat16)
    act_following = act_following.reshape(slots, half * chan_mid)
    act_rows = act_one[:, 0].reshape(slots, half * chan_mid)
    act_cols = act_one[:, :, 0, :].reshape(slots, half * chan_mid)
    act_source = jnp.concatenate([act_rows, act_cols, act_following], axis=0)
    south_act, east_act, diag_act = select_many(
        act_source,
        ((nearby[:, 6], offset), (nearby[:, 4], offset - slots), (nearby[:, 7], offset - slots)),
    )
    padded_two = assemble(
        act_one,
        south_act.reshape(slots, half, chan_mid),
        east_act.reshape(slots, half, chan_mid),
        diag_act[:, :chan_mid],
    )
    normed_two, inverse_two = norm_forward(conv_forward(padded_two, weight_two))
    hidden_two = normed_two * gain_two
    factor = 1.0 / math.sqrt(lax.axis_size("dp") * lax.axis_size(SPACE) * slots * quarter * quarter)
    grad_out = cotangent[0].reshape(slots, quarter, quarter, chan_out).astype(jnp.float32)
    grad_out = jnp.where(live[:, None, None, None], grad_out * factor, jnp.zeros_like(grad_out))
    grad_z_two, grad_gain_two = norm_backward(
        grad_out, hidden_two, normed_two, inverse_two, gain_two
    )
    grad_z_two = grad_z_two.astype(jnp.bfloat16)
    grad_weight_two = weight_grad(padded_two, grad_z_two)
    grad_padded = input_grad(grad_z_two, weight_two)
    bottom = grad_padded[:, half, :half, :].astype(jnp.bfloat16).reshape(slots, half * chan_mid)
    right = grad_padded[:, :, half, :].astype(jnp.bfloat16).reshape(slots, (half + 1) * chan_mid)
    previous = from_behind(right, SPACE, 1)
    bottom_wide = jnp.concatenate([bottom, jnp.zeros((slots, chan_mid), bottom.dtype)], axis=1)
    rim_source = jnp.concatenate([previous, right, bottom_wide], axis=0)
    from_west, from_diag, from_north = select_many(
        rim_source,
        (
            (nearby[:, 3], offset - slots),
            (nearby[:, 0], offset - slots),
            (nearby[:, 1], offset - 2 * slots),
        ),
    )
    from_west = from_west.reshape(slots, half + 1, chan_mid)
    from_diag = from_diag.reshape(slots, half + 1, chan_mid)
    from_north = from_north[:, : half * chan_mid].reshape(slots, half, chan_mid)
    base = grad_padded[:, :half, :half, :]
    inner = ((jnp.arange(half) > 0)[:, None] & (jnp.arange(half) > 0)[None, :])[None, :, :, None]
    inner_z, inner_gain = norm_backward(
        jnp.where(inner, base, 0.0), jnp.where(inner, hidden_one, 0.0), normed_one, inverse_one, gain_one
    )
    inner_low = jnp.where(inner, inner_z, 0.0).astype(jnp.bfloat16)
    inner_weight = weight_grad(padded_one, inner_low)
    grad_act = base
    grad_act = grad_act.at[:, 0].add(from_north.astype(jnp.float32))
    grad_act = grad_act.at[:, :, 0].add(from_west[:, :half].astype(jnp.float32))
    grad_act = grad_act.at[:, 0, 0].add(from_diag[:, half].astype(jnp.float32))
    border_z, border_gain = norm_backward(
        jnp.where(inner, 0.0, grad_act), hidden_one, normed_one, inverse_one, gain_one
    )
    border_low = jnp.where(inner, 0.0, border_z).astype(jnp.bfloat16)
    top = weight_grad(padded_one[:, :3], border_low[:, :1])
    left = weight_grad(padded_one[:, 2:, :3], border_low[:, 1:, :1])
    grad_weight_one = inner_weight + top + left
    grad_gain_one = inner_gain + border_gain
    parts = (grad_weight_one, grad_weight_two, grad_gain_one, grad_gain_two)
    flat = jnp.concatenate([part.reshape(-1) for part in parts])
    flat = summed_everywhere(flat, ("dp", "space_0"), ("space_1", "space_2"))
    sizes = [part.size for part in parts]
    bounds = [sum(sizes[:index]) for index in range(len(sizes) + 1)]
    grad_weight_one, grad_weight_two, grad_gain_one, grad_gain_two = (
        flat[start:end].reshape(part.shape)
        for start, end, part in zip(bounds[:-1], bounds[1:], parts)
    )
    return (grad_weight_one, grad_weight_two, grad_gain_one, grad_gain_two)


def solution(mesh):
    torus = Mesh(
        mesh.devices.reshape(mesh.shape["dp"], 8, 4, 2), ("dp", "space_0", "space_1", "space_2")
    )
    return jax.shard_map(
        on_device,
        mesh=torus,
        in_specs=(
            P("dp", SPACE, None, None),
            P("dp", SPACE, None, None),
            P("dp", SPACE),
            P("dp", SPACE, None),
            P(),
            P(),
            P(),
            P(),
        ),
        out_specs=(P(), P(), P(), P()),
        check_vma=False,
    )
```

```python
import math

import jax
import jax.numpy as jnp
from jax import lax
from jax.sharding import Mesh
from jax.sharding import PartitionSpec as P

SPACE = ("space_0", "space_1", "space_2")


EPS = 1e-05


def from_behind(value, axis, steps):
    count = lax.axis_size(axis)
    first, last = (max(0, -steps), min(count, count - steps))
    return lax.ppermute(value, axis, [(source, source + steps) for source in range(first, last)])


def cut_along(value, dim, peers):
    before, after = (value.shape[:dim], value.shape[dim + 1 :])
    return jnp.moveaxis(value.reshape(*before, peers, -1, *after), dim, 0)


def sent_and_summed(value, axis, dim):
    peers = lax.axis_size(axis)
    pieces = lax.all_to_all(cut_along(value, dim, peers), axis, 0, 0, tiled=True)
    return jnp.sum(pieces, axis=0)


def summed_rows(value, axes, dim):
    far, near = axes
    pieces = cut_along(value, dim, lax.axis_size(far))
    nearer = sent_and_summed(pieces, near, dim + 1)
    arrived = lax.all_to_all(nearer, far, split_axis=0, concat_axis=0, tiled=True)
    return arrived.sum(axis=0)


def rows_for(lines, peers):
    spare = -lines.shape[0] % peers
    if not spare:
        return lines
    return jnp.concatenate([lines, jnp.zeros((spare, *lines.shape[1:]), lines.dtype)])


def from_everyone(value, axis):
    peers = lax.axis_size(axis)
    return lax.all_to_all(
        jnp.broadcast_to(value[None], (peers, *value.shape)), axis, 0, 0, tiled=True
    )


def in_order(pieces, dim):
    pieces = jnp.moveaxis(pieces, 0, dim)
    dims = pieces.shape
    return pieces.reshape(*dims[:dim], dims[dim] * dims[dim + 1], *dims[dim + 2 :])


def gathered_by_axis(value, axes, dim):
    far, near = axes
    first = from_everyone(value, far)
    pieces = jnp.swapaxes(from_everyone(first, near), 0, 1)
    return in_order(pieces.reshape(-1, *value.shape), dim)


def total_of(value, axes):
    lines = value.reshape(-1)
    own = summed_rows(rows_for(lines, lax.axis_size(axes[0]) * lax.axis_size(axes[1])), axes, 0)
    whole = gathered_by_axis(own, axes, 0)
    return whole[: len(lines)].reshape(value.shape)


def summed_everywhere(value, far, near):
    lines = rows_for(value, lax.axis_size(far) * lax.axis_size(near))
    far_peers = lax.axis_size(far)
    mine = lax.all_to_all(lines.reshape(far_peers, -1), far, 0, 0, tiled=True).sum(axis=0)
    mine = from_everyone(mine, near).sum(axis=0)
    return from_everyone(mine, far).reshape(-1)[: value.shape[0]]


def norm_forward(values):
    middle = jnp.mean(values, axis=-1, keepdims=True)
    centred = values - middle
    inverse = lax.rsqrt(jnp.mean(centred * centred, axis=-1, keepdims=True) + EPS)
    return (centred * inverse, inverse)


def norm_backward(grad_act, hidden, normed, inverse, gain):
    sig = jax.nn.sigmoid(hidden)
    grad_hidden = grad_act * sig * (1.0 + hidden * (1.0 - sig))
    grad_gain = jnp.sum(grad_hidden * normed, axis=(0, 1, 2))
    scaled = grad_hidden * gain
    centre = jnp.mean(scaled, axis=-1, keepdims=True)
    along = jnp.mean(scaled * normed, axis=-1, keepdims=True)
    return (inverse * (scaled - centre - normed * along), grad_gain)


def select_rows(source, idents, offset):
    positions = jnp.clip(idents - offset, 0, source.shape[0] - 1)
    picked = jnp.take(source, positions, axis=0)
    return jnp.where((idents >= 0)[:, None], picked, jnp.zeros_like(picked))


def select_many(source, requests):
    idents = jnp.concatenate([wanted for wanted, _ in requests])
    shifts = jnp.concatenate([jnp.full(wanted.shape, shift) for wanted, shift in requests])
    picked = select_rows(source, idents, shifts)
    return jnp.split(picked, len(requests))


def assemble(field, south_rows, east_cols, corners):
    lower = jnp.concatenate([field, south_rows[:, None]], axis=1)
    right = jnp.concatenate([east_cols, corners[:, None]], axis=1)
    return jnp.concatenate([lower, right[:, :, None]], axis=2)


def conv_forward(padded, weight):
    return lax.conv_general_dilated(
        padded,
        weight,
        (2, 2),
        "VALID",
        dimension_numbers=("NHWC", "HWIO", "NHWC"),
        preferred_element_type=jnp.float32,
    )


def weight_grad(padded, grad_z):
    return lax.conv_general_dilated(
        padded,
        grad_z,
        (1, 1),
        "VALID",
        rhs_dilation=(2, 2),
        dimension_numbers=("CHWN", "IHWO", "HWNC"),
        preferred_element_type=jnp.float32,
    )


def input_grad(grad_z, weight):
    return lax.conv_general_dilated(
        grad_z,
        weight[::-1, ::-1],
        (1, 1),
        ((2, 2), (2, 2)),
        lhs_dilation=(2, 2),
        dimension_numbers=("NHWC", "HWOI", "NHWC"),
        preferred_element_type=jnp.float32,
    )


def on_device(image, cotangent, live_count, neighbours, weight_one, weight_two, gain_one, gain_two):
    slots = image.shape[1]
    tile = image.shape[2]
    chan_in = weight_one.shape[2]
    chan_mid = weight_one.shape[3]
    chan_out = weight_two.shape[3]
    half = tile // 2
    quarter = tile // 4
    offset = lax.axis_index(SPACE) * slots
    nearby = neighbours[0]
    live = jnp.arange(slots) < live_count[0, 0]
    field = image[0].reshape(slots, tile, tile, chan_in)
    field = jnp.where(live[:, None, None, None], field, jnp.zeros_like(field))
    image_rows = field[:, 0].reshape(slots, tile * chan_in)
    south_image = select_rows(image_rows, nearby[:, 6], offset).reshape(slots, 1, tile, chan_in)
    strip = jnp.concatenate([field, south_image], axis=1)[:, :, :3, :]
    strip_following = from_behind(strip, SPACE, -1)
    image_cols = field[:, :, 0, :].reshape(slots, tile * chan_in)
    following = strip_following[:, :tile, 0, :].reshape(slots, tile * chan_in)
    source = jnp.concatenate([image_cols, following], axis=0)
    east_image, diag_image = select_many(
        source, ((nearby[:, 4], offset), (nearby[:, 7], offset))
    )
    padded_one = assemble(
        field,
        south_image[:, 0],
        east_image.reshape(slots, tile, chan_in),
        diag_image[:, :chan_in],
    )
    normed_one, inverse_one = norm_forward(conv_forward(padded_one, weight_one))
    hidden_one = normed_one * gain_one
    act_one = jax.nn.silu(hidden_one).astype(jnp.bfloat16)
    normed_edge, _ = norm_forward(conv_forward(strip_following, weight_one))
    act_following = jax.nn.silu(normed_edge * gain_one).astype(jnp.bfloat16)
    act_following = act_following.reshape(slots, half * chan_mid)
    act_rows = act_one[:, 0].reshape(slots, half * chan_mid)
    act_cols = act_one[:, :, 0, :].reshape(slots, half * chan_mid)
    act_source = jnp.concatenate([act_rows, act_cols, act_following], axis=0)
    south_act, east_act, diag_act = select_many(
        act_source,
        ((nearby[:, 6], offset), (nearby[:, 4], offset - slots), (nearby[:, 7], offset - slots)),
    )
    padded_two = assemble(
        act_one,
        south_act.reshape(slots, half, chan_mid),
        east_act.reshape(slots, half, chan_mid),
        diag_act[:, :chan_mid],
    )
    normed_two, inverse_two = norm_forward(conv_forward(padded_two, weight_two))
    hidden_two = normed_two * gain_two
    factor = 1.0 / math.sqrt(lax.axis_size("dp") * lax.axis_size(SPACE) * slots * quarter * quarter)
    grad_out = cotangent[0].reshape(slots, quarter, quarter, chan_out).astype(jnp.float32)
    grad_out = jnp.where(live[:, None, None, None], grad_out * factor, jnp.zeros_like(grad_out))
    grad_z_two, grad_gain_two = norm_backward(
        grad_out, hidden_two, normed_two, inverse_two, gain_two
    )
    grad_z_two = grad_z_two.astype(jnp.bfloat16)
    grad_weight_two = weight_grad(padded_two, grad_z_two)
    grad_padded = input_grad(grad_z_two, weight_two)
    bottom = grad_padded[:, half, :half, :].astype(jnp.bfloat16).reshape(slots, half * chan_mid)
    right = grad_padded[:, :, half, :].astype(jnp.bfloat16).reshape(slots, (half + 1) * chan_mid)
    previous = from_behind(right, SPACE, 1)
    bottom_wide = jnp.concatenate([bottom, jnp.zeros((slots, chan_mid), bottom.dtype)], axis=1)
    rim_source = jnp.concatenate([previous, right, bottom_wide], axis=0)
    from_west, from_diag, from_north = select_many(
        rim_source,
        (
            (nearby[:, 3], offset - slots),
            (nearby[:, 0], offset - slots),
            (nearby[:, 1], offset - 2 * slots),
        ),
    )
    from_west = from_west.reshape(slots, half + 1, chan_mid)
    from_diag = from_diag.reshape(slots, half + 1, chan_mid)
    from_north = from_north[:, : half * chan_mid].reshape(slots, half, chan_mid)
    grad_act = grad_padded[:, :half, :half, :]
    grad_act = grad_act.at[:, 0].add(from_north.astype(jnp.float32))
    grad_act = grad_act.at[:, :, 0].add(from_west[:, :half].astype(jnp.float32))
    grad_act = grad_act.at[:, 0, 0].add(from_diag[:, half].astype(jnp.float32))
    grad_z_one, grad_gain_one = norm_backward(
        grad_act, hidden_one, normed_one, inverse_one, gain_one
    )
    grad_weight_one = weight_grad(padded_one, grad_z_one.astype(jnp.bfloat16))
    parts = (grad_weight_one, grad_weight_two, grad_gain_one, grad_gain_two)
    flat = jnp.concatenate([part.reshape(-1) for part in parts])
    flat = summed_everywhere(flat, ("space_0", "space_1"), ("dp", "space_2"))
    sizes = [part.size for part in parts]
    bounds = [sum(sizes[:index]) for index in range(len(sizes) + 1)]
    grad_weight_one, grad_weight_two, grad_gain_one, grad_gain_two = (
        flat[start:end].reshape(part.shape)
        for start, end, part in zip(bounds[:-1], bounds[1:], parts)
    )
    return (grad_weight_one, grad_weight_two, grad_gain_one, grad_gain_two)


def solution(mesh):
    torus = Mesh(
        mesh.devices.reshape(mesh.shape["dp"], 8, 4, 2), ("dp", "space_0", "space_1", "space_2")
    )
    return jax.shard_map(
        on_device,
        mesh=torus,
        in_specs=(
            P("dp", SPACE, None, None),
            P("dp", SPACE, None, None),
            P("dp", SPACE),
            P("dp", SPACE, None),
            P(),
            P(),
            P(),
            P(),
        ),
        out_specs=(P(), P(), P(), P()),
        check_vma=False,
    )
```
